32 devices in a mesh: groups: 2 (over y), seq: 4 (over z), fsdp: 4 (over x, core).
Axes of the slice: x: 2, y: 2, z: 4, core: 2. Of those that a mesh axis runs over, the one named last changes fastest.
Arguments:
- tokens: bfloat16 [1024, 1024], P(('groups', 'seq')), parts along dimension 0, may hold values from -16 to 16
- qkv_weight: bfloat16 [1024, 1536], P('seq', 'fsdp'), may hold values from -0.125 to 0.125
- covisible: int32 [8, 4], P('groups'), parts along dimension 0, may hold values 0 or 1
- block_drive: int32 [8], P('groups'), parts along dimension 0, may hold values from 0 to 2
- grad_out: bfloat16 [1024, 512], P(('groups', 'seq'), 'fsdp'), parts along dimension 0, may hold values from -6 to 6
Outputs:
- attention: bfloat16 [1024, 512], P(('groups', 'seq'), 'fsdp'), parts along dimension 0
- grad_input: bfloat16 [1024, 1024], P(('groups', 'seq'), 'fsdp'), parts along dimension 0
- grad_weight: float32 [2048, 1536], P(('groups', 'seq'), 'fsdp'), parts along dimension 0
The draws below stay inside these ranges and needn't reach their ends.
There are 2 independent parts, one for each index of `groups`. The reference program is written for one: setup_inputs(seed, part) draws one part's arguments, and reference() takes and returns one part's arrays. A program takes and returns all parts, laid end to end along the dimension named above; an argument that names none is the same for every part. Nothing has to cross between parts.
All inputs are finite; a program needn't handle non-finite values.
Results may differ from the reference program's by a relative error of at most 0.018.
The reference program's roundings to bfloat16 on the way count: a program that leaves them out, or rounds other values in their place, can miss the bound.
Values may be sent and summed in bfloat16 or wider, within the bound.
No kernel may reach another device: no remote copies, remote signals or barrier semaphores. Data moves between devices by JAX's collectives and lax.ppermute only.
A program may use at most 64 MiB of HBM per device.

```python
import math
import jax
import jax.numpy as jnp
from jax import lax

D = 1024
HD = 64
HEADS = 8
BLOCK = 128
TOKENS = 512
NBLK = 4


def draw_tokens(key, part):
    normal_part = jax.random.normal(jax.random.fold_in(key, 11), (TOKENS, D), jnp.float32)
    scales = jnp.exp(jax.random.uniform(jax.random.fold_in(key, 12), (TOKENS, 1), jnp.float32, 0.0, math.log(2.5)))
    values = scales * jnp.clip(normal_part, -4.0, 4.0)
    return values.astype(jnp.bfloat16)


def draw_qkv_weight(key, part):
    normal_part = jax.random.normal(jax.random.fold_in(key, 21), (D, HEADS, 3, HD), jnp.float32)
    normal_part = jnp.clip(normal_part, -4.0, 4.0) * D ** (-0.5)
    return normal_part.reshape(D, 3 * HEADS * HD).astype(jnp.bfloat16)


def plant(drawn, stream_key, smallest, high):
    longest = drawn.shape.index(max(drawn.shape))
    spots = []
    for shift in (0, 1):
        where = [jax.random.randint(jax.random.fold_in(stream_key, axis), (), 0, length) for axis, length in enumerate(drawn.shape)]
        where[longest] = (where[longest] + shift) % drawn.shape[longest]
        spots.append(tuple(where))
    return drawn.at[spots[0]].set(smallest).at[spots[1]].set(high)


def level_of(rng, shape, cuts, low, top_value):
    def one(position, shards_of):
        steps = jax.random.uniform(jax.random.fold_in(jax.random.fold_in(rng, 6), position), (shards_of,), jnp.float32, low / len(cuts), top_value / len(cuts))
        return jnp.repeat(jnp.exp(steps), shape[position] // shards_of).reshape((-1,) + (1,) * (len(shape) - position - 1))

    factor_of = one(*cuts[0])
    for cut in cuts[1:]:
        factor_of = factor_of * one(*cut)
    return factor_of


def scatter_about(stream_key, extent, spread, reach, shards=(), dtype=jnp.bfloat16):
    drawn = jax.random.normal(stream_key, extent, jnp.float32) * spread
    if len(shards) > 0:
        drawn = level_of(stream_key, extent, shards, -0.22, 0.18) * drawn
    return jnp.clip(drawn, min=-reach, max=reach).astype(dtype)


def setup_inputs(seed: int = 0, part: int = 0) -> dict:
    arg_keys = jax.random.split(jax.random.key(seed), 6)
    part_keys = jax.random.split(jax.random.fold_in(arg_keys[5], part), 6)
    tokens = draw_tokens(jax.random.fold_in(jax.random.fold_in(arg_keys[5], part), 71), part)
    qkv_weight = draw_qkv_weight(jax.random.fold_in(arg_keys[5], 71), part)
    covisible = plant((jax.random.randint(part_keys[2], (NBLK, NBLK), 0, 3) < 1).astype(jnp.int32), jax.random.fold_in(part_keys[2], 1), 0, 1)
    block_drive = plant(jax.random.randint(part_keys[3], (NBLK,), 0, 3), jax.random.fold_in(part_keys[3], 1), 0, 2).astype(jnp.int32)
    grad_out = scatter_about(part_keys[4], (TOKENS, HEADS * HD), 1.0, 6.0, ((0, 4), (1, 4)))
    return dict(tokens=tokens, qkv_weight=qkv_weight, covisible=covisible, block_drive=block_drive, grad_out=grad_out)


MASKED_SCORE = -1.0e30


def reference(tokens, qkv_weight, covisible, block_drive, grad_out):
    scaling = HD ** -0.5
    projected = jnp.dot(tokens, qkv_weight, preferred_element_type=jnp.float32).astype(jnp.bfloat16)
    projected = projected.reshape(TOKENS, HEADS, 3, HD)
    all_queries = jnp.transpose(projected[:, :, 0, :], (1, 0, 2))
    all_keys = jnp.transpose(projected[:, :, 1, :], (1, 0, 2))
    all_values = jnp.transpose(projected[:, :, 2, :], (1, 0, 2))
    all_grads = jnp.transpose(grad_out.reshape(TOKENS, HEADS, HD), (1, 0, 2))
    allowed = jnp.logical_or(covisible == 1, block_drive[:, None] == block_drive[None, :])
    token_block = lax.iota(jnp.int32, TOKENS) // BLOCK
    key_allowed = jnp.take(allowed, token_block, axis=1)
    block_rows = math.gcd(TOKENS, 512)
    visits = TOKENS // block_rows

    def one_head(operands):
        head_queries, head_keys, head_values, head_grads = operands
        wide_values = head_values.astype(jnp.float32)

        def visit(carried, block_index):
            grad_keys, grad_values = carried
            first_row = (block_index * block_rows).astype(jnp.int32)
            row_queries = lax.dynamic_slice_in_dim(head_queries, first_row, block_rows, 0)
            row_grads = lax.dynamic_slice_in_dim(head_grads, first_row, block_rows, 0)
            row_blocks = lax.dynamic_slice_in_dim(token_block, first_row, block_rows, 0)
            visible = jnp.take(key_allowed, row_blocks, axis=0)
            scores = jnp.dot(row_queries, head_keys.T, preferred_element_type=jnp.float32) * scaling
            row_max = jnp.where(visible, scores, MASKED_SCORE).max(axis=1)
            row_sum = jnp.sum(jnp.exp(jnp.where(visible, scores - row_max[:, None], MASKED_SCORE)), axis=1)
            log_total = row_max + jnp.log(row_sum)
            probabilities = jnp.exp(jnp.where(visible, scores - log_total[:, None], MASKED_SCORE))
            rounded_prob = probabilities.astype(jnp.bfloat16)
            attention_rows = jnp.dot(probabilities, wide_values, precision=lax.Precision.HIGHEST, preferred_element_type=jnp.float32).astype(jnp.bfloat16)
            grad_dot = jnp.sum(row_grads.astype(jnp.float32) * attention_rows.astype(jnp.float32), axis=1)
            grad_prob = jnp.dot(row_grads, head_values.T, preferred_element_type=jnp.float32)
            grad_score = (probabilities * (grad_prob - grad_dot[:, None]) * scaling).astype(jnp.bfloat16)
            grad_rows = jnp.dot(grad_score, head_keys, preferred_element_type=jnp.float32)
            grad_keys = grad_keys + jnp.dot(grad_score.T, row_queries, preferred_element_type=jnp.float32)
            grad_values = grad_values + jnp.dot(rounded_prob.T, row_grads, preferred_element_type=jnp.float32)
            return (grad_keys, grad_values), (attention_rows, grad_rows)

        zero_grads = jnp.zeros((TOKENS, HD), jnp.float32)
        (grad_keys, grad_values), (attention_rows, grad_rows) = lax.scan(visit, (zero_grads, zero_grads), lax.iota(jnp.int32, visits))
        return attention_rows.reshape(TOKENS, HD), grad_rows.reshape(TOKENS, HD), grad_keys, grad_values

    attention_heads, grad_queries, grad_keys, grad_values = lax.map(one_head, (all_queries, all_keys, all_values, all_grads))
    attention = jnp.transpose(attention_heads, (1, 0, 2)).reshape(TOKENS, HEADS * HD)
    stacked = jnp.stack([grad_queries, grad_keys, grad_values], axis=2)
    grad_qkv = jnp.transpose(stacked, (1, 0, 2, 3)).reshape(TOKENS, 3 * HEADS * HD).astype(jnp.bfloat16)
    grad_input = jnp.dot(grad_qkv, qkv_weight.T, preferred_element_type=jnp.float32).astype(jnp.bfloat16)
    grad_weight = jnp.dot(tokens.T, grad_qkv, preferred_element_type=jnp.float32) * (TOKENS ** -0.5)
    return attention, grad_input, grad_weight
```

```python
import functools
import jax
import jax.numpy as jnp
from jax import lax
from jax.experimental import pallas as pl
from jax.experimental.pallas import tpu as pltpu
from jax.sharding import PartitionSpec as P

HD = 64
BLOCK = 128
MASKED_SCORE = -1e30
BF = jnp.bfloat16
F32 = jnp.float32


def query_visible(covisible, block_drive, first_block, block_count):
    own_rows = lax.dynamic_slice_in_dim(covisible, first_block, block_count, 0)
    own_drive = lax.dynamic_slice_in_dim(block_drive, first_block, block_count, 0)
    joined = jnp.logical_or(own_rows == 1, own_drive[:, None] == block_drive[None, :])
    return joined.astype(jnp.float32)


def key_visible(covisible, block_drive, first_block, block_count):
    own_columns = lax.dynamic_slice_in_dim(covisible, first_block, block_count, 1)
    own_drive = lax.dynamic_slice_in_dim(block_drive, first_block, block_count, 0)
    joined = jnp.logical_or(own_columns == 1, block_drive[:, None] == own_drive[None, :])
    return joined.astype(jnp.float32)


def block_onehot(length, block_total):
    member = lax.iota(jnp.int32, length) // BLOCK
    return (member[:, None] == lax.iota(jnp.int32, block_total)[None, :]).astype(jnp.float32)


def general(tokens, qkv_weight, covisible, block_drive, grad_out):
    local_rows = tokens.shape[0]
    seq_count = lax.axis_size("seq")
    seq_index = lax.axis_index("seq")
    out_width = qkv_weight.shape[1]
    local_heads = out_width // (3 * HD)
    block_count = local_rows // BLOCK
    block_total = covisible.shape[0]
    first_block = seq_index * block_count
    scaling = HD ** (-0.5)
    rows_visible = query_visible(covisible, block_drive, first_block, block_count)
    columns_visible = key_visible(covisible, block_drive, first_block, block_count)
    weight = lax.all_gather(qkv_weight, "seq", axis=0, tiled=True)
    projected = jnp.dot(tokens, weight, preferred_element_type=jnp.float32)
    projected = projected.astype(jnp.bfloat16).reshape(local_rows, local_heads, 3, HD)
    queries = projected[:, :, 0, :]
    local_keys = projected[:, :, 1, :]
    local_values = projected[:, :, 2, :]
    key_value = projected[:, :, 1:, :].reshape(local_rows, local_heads * 2 * HD)
    panel = lax.all_gather(key_value, "seq", axis=0, tiled=True)
    length = panel.shape[0]
    onehot = block_onehot(length, block_total)
    visible = (jnp.repeat(jnp.dot(rows_visible, onehot.T), BLOCK, axis=0) > 0.5)[None]
    split_panel = panel.reshape(length, local_heads, 2, HD)
    panel_keys = split_panel[:, :, 0, :]
    scores = (
        jnp.einsum("qhd,khd->hqk", queries, panel_keys, preferred_element_type=jnp.float32)
        * scaling
    )
    running_max = jnp.where(visible, scores, MASKED_SCORE).max(axis=2)
    shifted = jnp.exp(jnp.where(visible, scores - running_max[:, :, None], MASKED_SCORE))
    running_sum = shifted.sum(axis=2)
    wide_values = split_panel[:, :, 1, :].astype(jnp.float32)
    weighted = jnp.einsum(
        "hqk,khd->hqd",
        shifted,
        wide_values,
        precision=lax.Precision.HIGHEST,
        preferred_element_type=jnp.float32,
    )
    attention_heads = (weighted / running_sum[:, :, None]).astype(jnp.bfloat16)
    attention = jnp.transpose(attention_heads, (1, 0, 2)).reshape(local_rows, local_heads * HD)
    log_total = running_max + jnp.log(running_sum)
    grad_heads = grad_out.reshape(local_rows, local_heads, HD)
    grad_dot_rows = jnp.sum(
        grad_heads.astype(jnp.float32)
        * attention.reshape(local_rows, local_heads, HD).astype(jnp.float32),
        axis=2,
    )
    grad_dot = jnp.transpose(grad_dot_rows)
    log_total_rows = jnp.transpose(log_total)
    all_log_total = lax.all_gather(log_total_rows, "seq", axis=0, tiled=True)
    all_grad_dot = lax.all_gather(grad_dot_rows, "seq", axis=0, tiled=True)
    query_rows = queries.reshape(local_rows, local_heads * HD)
    far_queries = lax.all_gather(query_rows, "seq", axis=0, tiled=True)
    far_grads = lax.all_gather(grad_out, "seq", axis=0, tiled=True)
    visible_columns = (jnp.repeat(jnp.dot(onehot, columns_visible), BLOCK, axis=1) > 0.5)[None]
    far_heads = far_queries.reshape(length, local_heads, HD)
    far_grad_heads = far_grads.reshape(length, local_heads, HD)
    far_log_total = jnp.transpose(all_log_total)
    far_grad_dot = jnp.transpose(all_grad_dot)
    scores = (
        jnp.einsum("qhd,khd->hqk", far_heads, local_keys, preferred_element_type=jnp.float32)
        * scaling
    )
    probabilities = jnp.exp(
        jnp.where(visible_columns, scores - far_log_total[:, :, None], MASKED_SCORE)
    )
    grad_prob = jnp.einsum(
        "qhd,khd->hqk", far_grad_heads, local_values, preferred_element_type=jnp.float32
    )
    grad_score = (probabilities * (grad_prob - far_grad_dot[:, :, None]) * scaling).astype(
        jnp.bfloat16
    )
    grad_keys = jnp.einsum(
        "hqk,qhd->khd", grad_score, far_heads, preferred_element_type=jnp.float32
    )
    grad_values = jnp.einsum(
        "hqk,qhd->khd",
        probabilities.astype(jnp.bfloat16),
        far_grad_heads,
        preferred_element_type=jnp.float32,
    )
    scores = (
        jnp.einsum("qhd,khd->hqk", queries, panel_keys, preferred_element_type=jnp.float32)
        * scaling
    )
    probabilities = jnp.exp(jnp.where(visible, scores - log_total[:, :, None], MASKED_SCORE))
    grad_prob = jnp.einsum(
        "qhd,khd->hqk", grad_heads, split_panel[:, :, 1, :], preferred_element_type=jnp.float32
    )
    grad_score = (probabilities * (grad_prob - grad_dot[:, :, None]) * scaling).astype(jnp.bfloat16)
    grad_queries = jnp.einsum(
        "hqk,khd->qhd", grad_score, panel_keys, preferred_element_type=jnp.float32
    )
    grad_qkv = (
        jnp.stack([grad_queries, grad_keys, grad_values], axis=2)
        .astype(jnp.bfloat16)
        .reshape(local_rows, out_width)
    )
    partial_input = lax.dot_general(
        grad_qkv, weight, (((1,), (1,)), ((), ())), preferred_element_type=jnp.float32
    )
    grad_input = lax.psum_scatter(partial_input, "fsdp", scatter_dimension=1, tiled=True).astype(
        jnp.bfloat16
    )
    token_scale = (local_rows * seq_count) ** (-0.5)
    column_tokens = lax.all_to_all(tokens, "seq", split_axis=1, concat_axis=0, tiled=True)
    summed_rows = lax.dot_general(
        column_tokens,
        lax.all_gather(grad_qkv, "seq", axis=0, tiled=True),
        (((0,), (0,)), ((), ())),
        preferred_element_type=jnp.float32,
    )
    return (attention, grad_input, summed_rows * token_scale)


def dot(a, b):
    return lax.dot_general(a, b, (((1,), (0,)), ((), ())), preferred_element_type=F32)


def dot_nt(a, b):
    return lax.dot_general(a, b, (((1,), (1,)), ((), ())), preferred_element_type=F32)


def heads_kernel(slots, refs_of, *refs):
    named = dict(zip(refs_of, refs))
    covis, drive = named["covis"], named["drive"]
    t_all, w_all, gq = named["t_all"], named["w_all"], named["gq"]
    rows = BLOCK
    length = slots * rows
    z = lax.axis_index("seq")
    f = lax.axis_index("fsdp")
    y = lax.axis_index("groups")
    depth = w_all.shape[0] // slots
    half = depth // 2
    quarter = t_all.shape[1] // 4

    t_all[0:rows, :] = named["t0"][...]
    w_all[pl.ds(pl.multiple_of(z * depth, depth), depth), :] = named["w0"][...]
    width = w_all.shape[1]
    for k in range(1, slots):
        block = named["r%d" % k]
        first = (z ^ k) * depth
        w_all[pl.ds(pl.multiple_of(first + y * half, half), half), :] = block[:, 0:width]
        w_all[pl.ds(pl.multiple_of(first + (1 - y) * half, half), half), :] = named["v%d" % k][...]
        here = pl.ds(k * rows, rows)
        t_all[here, pl.ds(pl.multiple_of(f * quarter, quarter), quarter)] = block[
            :, width : width + quarter
        ]
        for m in range(1, 4):
            t_all[here, pl.ds(pl.multiple_of((f ^ m) * quarter, quarter), quarter)] = named[
                "t%d_%d" % (k, m)
            ][...]
    grads = jnp.concatenate(
        [named["g0"][...]] + [named["r%d" % k][:, width + quarter :] for k in range(1, slots)],
        axis=0,
    )
    projected = dot(t_all[...], w_all[...]).astype(BF)
    grads_t = jnp.transpose(grads)

    bias = {}
    for a in range(slots):
        for b in range(slots):
            i, j = z ^ a, z ^ b
            seen = jnp.logical_or(covis[i, j] == 1, drive[i] == drive[j])
            bias[a, b] = jnp.where(seen, 0.0, MASKED_SCORE).astype(F32)

    heads = width // (3 * HD)
    span = 2 * rows
    out_columns = []
    attention_t = []
    for h in range(heads):
        base = 3 * HD * h
        q8 = projected[:, base : base + HD] * jnp.asarray(HD ** (-0.5), BF)
        k_h = projected[:, base + HD : base + 2 * HD]
        v_h = projected[:, base + 2 * HD : base + 3 * HD]
        k_t = jnp.transpose(k_h)
        v_t = jnp.transpose(v_h)
        g_h = grads[:, HD * h : HD * (h + 1)]
        g_t = grads_t[HD * h : HD * (h + 1), :]
        d_k = jnp.zeros((length, HD), F32)
        d_v = jnp.zeros((length, HD), F32)
        d_q_t = []
        for part in range(length // span):
            at = slice(part * span, (part + 1) * span)
            s_t = dot_nt(k_h, q8[at])
            masked = []
            for b in range(slots):
                masked.append(
                    jnp.concatenate(
                        [
                            s_t[b * rows : (b + 1) * rows, e * rows : (e + 1) * rows]
                            + bias[part * 2 + e, b]
                            for e in range(span // rows)
                        ],
                        axis=1,
                    )
                )
            s_t = jnp.concatenate(masked, axis=0)
            top = jnp.max(s_t, axis=0, keepdims=True)
            e_t = jnp.exp(s_t - top)
            total = jnp.sum(e_t, axis=0, keepdims=True)
            p_t = e_t * (1.0 / total)
            p_b = p_t.astype(BF)
            p_rest = (p_t - p_b.astype(F32)).astype(BF)
            o_t = (dot(v_t, p_b) + dot(v_t, p_rest)).astype(BF)
            if part == 0:
                attention_t.append(o_t[:, 0:rows])
            grad_dot = jnp.sum(
                g_t[:, at].astype(F32) * o_t.astype(F32), axis=0, keepdims=True
            )
            dp_t = dot_nt(v_h, g_h[at])
            ds_t = (p_t * (dp_t - grad_dot)).astype(BF)
            d_v = d_v + dot(p_b, g_h[at])
            d_k = d_k + dot(ds_t, q8[at])
            d_q_t.append(dot(k_t, ds_t))
        d_q = jnp.transpose(jnp.concatenate(d_q_t, axis=1)) * (HD ** (-0.5))
        out_columns += [d_q, d_k, d_v]
    grad_qkv = jnp.concatenate(out_columns, axis=1).astype(BF)
    gq[...] = grad_qkv
    named["attention"][...] = jnp.transpose(jnp.concatenate(attention_t, axis=0))
    own = grad_qkv[0:rows]
    for m in range(4):
        out = named["part%d" % m]
        w_rows = w_all[pl.ds(pl.multiple_of((f ^ m) * depth, depth), depth), :]
        out[...] = dot_nt(own, w_rows).astype(out.dtype)
    named["t_d"][...] = t_all[:, pl.ds(pl.multiple_of(z * depth, depth), depth)]


def short(tokens, qkv_weight, covisible, block_drive, grad_out):
    rows, features = tokens.shape
    slots = lax.axis_size("seq")
    z = lax.axis_index("seq")
    f = lax.axis_index("fsdp")
    y = lax.axis_index("groups")
    depth, width = qkv_weight.shape
    quarter = features // 4
    half = depth // 2

    def swap(x, axis, bit):
        n = lax.axis_size(axis)
        return lax.ppermute(x, axis, [(i, i ^ bit) for i in range(n)])

    packed = jnp.concatenate(
        [
            lax.dynamic_slice_in_dim(qkv_weight, y * half, half, 0),
            lax.dynamic_slice_in_dim(tokens, f * quarter, quarter, 1),
            grad_out,
        ],
        axis=1,
    )
    got = {}
    got[2] = swap(packed, "seq", 2)
    got[1] = swap(packed, "seq", 1)
    got[3] = swap(got[2], "seq", 1)
    names, values = ["covis", "drive", "t0", "w0", "g0"], []
    values = [covisible, block_drive, tokens, qkv_weight, grad_out]
    for k in (2, 1, 3):
        piece = got[k][:, width : width + quarter]
        far = swap(piece, "fsdp", 2)
        names += ["r%d" % k, "v%d" % k, "t%d_1" % k, "t%d_2" % k, "t%d_3" % k]
        values += [
            got[k],
            swap(got[k][:, :width], "groups", 1),
            swap(piece, "fsdp", 1),
            far,
            swap(far, "fsdp", 1),
        ]
    outs = [
        ("attention", (rows, grad_out.shape[1]), BF),
        ("gq", (rows * slots, width), BF),
        ("t_d", (rows * slots, depth), BF),
        ("part0", (rows, depth), F32),
        ("part1", (rows, depth), BF),
        ("part2", (rows, depth), BF),
        ("part3", (rows, depth), BF),
    ]
    scratch = [
        ("t_all", pltpu.VMEM((rows * slots, features), BF)),
        ("w_all", pltpu.VMEM((depth * slots, width), BF)),
    ]
    vmem = pl.BlockSpec(memory_space=pltpu.VMEM)
    smem = pl.BlockSpec(memory_space=pltpu.SMEM)
    refs_of = names + [n for n, _, _ in outs] + [n for n, _ in scratch]
    attention, gq, t_d, *parts = pl.pallas_call(
        functools.partial(heads_kernel, slots, refs_of),
        out_shape=[jax.ShapeDtypeStruct(s, d) for _, s, d in outs],
        in_specs=[smem, smem] + [vmem] * (len(names) - 2),
        out_specs=[vmem] * len(outs),
        scratch_shapes=[s for _, s in scratch],
        compiler_params=pltpu.CompilerParams(vmem_limit_bytes=48 << 20),
        name="heads",
    )(*values)
    total = parts[0]
    for m in (1, 2, 3):
        total = total + swap(parts[m], "fsdp", m).astype(F32)
    grad_input = total.astype(BF)
    grad_weight = lax.dot_general(
        t_d, gq, (((0,), (0,)), ((), ())), preferred_element_type=F32
    ) * ((rows * slots) ** (-0.5))
    return attention, grad_input, grad_weight


def per_device(tokens, qkv_weight, covisible, block_drive, grad_out):
    rows, features = tokens.shape
    depth = qkv_weight.shape[0]
    fits = (
        lax.axis_size("seq") == 4
        and lax.axis_size("fsdp") == 4
        and lax.axis_size("groups") == 2
        and rows == BLOCK
        and depth * 4 == features
        and depth == 2 * rows
    )
    body = short if fits else general
    return body(tokens, qkv_weight, covisible, block_drive, grad_out)


def solution(mesh):
    in_specs = (
        P(("groups", "seq"), None),
        P("seq", "fsdp"),
        P("groups", None),
        P("groups"),
        P(("groups", "seq"), "fsdp"),
    )
    out_specs = (
        P(("groups", "seq"), "fsdp"),
        P(("groups", "seq"), "fsdp"),
        P(("groups", "seq"), "fsdp"),
    )
    return jax.shard_map(
        per_device, mesh=mesh, in_specs=in_specs, out_specs=out_specs, check_vma=False
    )
```

```python
import functools
import jax
import jax.numpy as jnp
from jax import lax
from jax.experimental import pallas as pl
from jax.experimental.pallas import tpu as pltpu
from jax.sharding import PartitionSpec as P

HD = 64
BLOCK = 128
MASKED_SCORE = -1e30
BF = jnp.bfloat16
F32 = jnp.float32


def query_visible(covisible, block_drive, first_block, block_count):
    own_rows = lax.dynamic_slice_in_dim(covisible, first_block, block_count, 0)
    own_drive = lax.dynamic_slice_in_dim(block_drive, first_block, block_count, 0)
    joined = jnp.logical_or(own_rows == 1, own_drive[:, None] == block_drive[None, :])
    return joined.astype(jnp.float32)


def key_visible(covisible, block_drive, first_block, block_count):
    own_columns = lax.dynamic_slice_in_dim(covisible, first_block, block_count, 1)
    own_drive = lax.dynamic_slice_in_dim(block_drive, first_block, block_count, 0)
    joined = jnp.logical_or(own_columns == 1, block_drive[:, None] == own_drive[None, :])
    return joined.astype(jnp.float32)


def block_onehot(length, block_total):
    member = lax.iota(jnp.int32, length) // BLOCK
    return (member[:, None] == lax.iota(jnp.int32, block_total)[None, :]).astype(jnp.float32)


def general(tokens, qkv_weight, covisible, block_drive, grad_out):
    local_rows = tokens.shape[0]
    seq_count = lax.axis_size("seq")
    seq_index = lax.axis_index("seq")
    out_width = qkv_weight.shape[1]
    local_heads = out_width // (3 * HD)
    block_count = local_rows // BLOCK
    block_total = covisible.shape[0]
    first_block = seq_index * block_count
    scaling = HD ** (-0.5)
    rows_visible = query_visible(covisible, block_drive, first_block, block_count)
    columns_visible = key_visible(covisible, block_drive, first_block, block_count)
    weight = lax.all_gather(qkv_weight, "seq", axis=0, tiled=True)
    projected = jnp.dot(tokens, weight, preferred_element_type=jnp.float32)
    projected = projected.astype(jnp.bfloat16).reshape(local_rows, local_heads, 3, HD)
    queries = projected[:, :, 0, :]
    local_keys = projected[:, :, 1, :]
    local_values = projected[:, :, 2, :]
    key_value = projected[:, :, 1:, :].reshape(local_rows, local_heads * 2 * HD)
    panel = lax.all_gather(key_value, "seq", axis=0, tiled=True)
    length = panel.shape[0]
    onehot = block_onehot(length, block_total)
    visible = (jnp.repeat(jnp.dot(rows_visible, onehot.T), BLOCK, axis=0) > 0.5)[None]
    split_panel = panel.reshape(length, local_heads, 2, HD)
    panel_keys = split_panel[:, :, 0, :]
    scores = (
        jnp.einsum("qhd,khd->hqk", queries, panel_keys, preferred_element_type=jnp.float32)
        * scaling
    )
    running_max = jnp.where(visible, scores, MASKED_SCORE).max(axis=2)
    shifted = jnp.exp(jnp.where(visible, scores - running_max[:, :, None], MASKED_SCORE))
    running_sum = shifted.sum(axis=2)
    wide_values = split_panel[:, :, 1, :].astype(jnp.float32)
    weighted = jnp.einsum(
        "hqk,khd->hqd",
        shifted,
        wide_values,
        precision=lax.Precision.HIGHEST,
        preferred_element_type=jnp.float32,
    )
    attention_heads = (weighted / running_sum[:, :, None]).astype(jnp.bfloat16)
    attention = jnp.transpose(attention_heads, (1, 0, 2)).reshape(local_rows, local_heads * HD)
    log_total = running_max + jnp.log(running_sum)
    grad_heads = grad_out.reshape(local_rows, local_heads, HD)
    grad_dot_rows = jnp.sum(
        grad_heads.astype(jnp.float32)
        * attention.reshape(local_rows, local_heads, HD).astype(jnp.float32),
        axis=2,
    )
    grad_dot = jnp.transpose(grad_dot_rows)
    log_total_rows = jnp.transpose(log_total)
    all_log_total = lax.all_gather(log_total_rows, "seq", axis=0, tiled=True)
    all_grad_dot = lax.all_gather(grad_dot_rows, "seq", axis=0, tiled=True)
    query_rows = queries.reshape(local_rows, local_heads * HD)
    far_queries = lax.all_gather(query_rows, "seq", axis=0, tiled=True)
    far_grads = lax.all_gather(grad_out, "seq", axis=0, tiled=True)
    visible_columns = (jnp.repeat(jnp.dot(onehot, columns_visible), BLOCK, axis=1) > 0.5)[None]
    far_heads = far_queries.reshape(length, local_heads, HD)
    far_grad_heads = far_grads.reshape(length, local_heads, HD)
    far_log_total = jnp.transpose(all_log_total)
    far_grad_dot = jnp.transpose(all_grad_dot)
    scores = (
        jnp.einsum("qhd,khd->hqk", far_heads, local_keys, preferred_element_type=jnp.float32)
        * scaling
    )
    probabilities = jnp.exp(
        jnp.where(visible_columns, scores - far_log_total[:, :, None], MASKED_SCORE)
    )
    grad_prob = jnp.einsum(
        "qhd,khd->hqk", far_grad_heads, local_values, preferred_element_type=jnp.float32
    )
    grad_score = (probabilities * (grad_prob - far_grad_dot[:, :, None]) * scaling).astype(
        jnp.bfloat16
    )
    grad_keys = jnp.einsum(
        "hqk,qhd->khd", grad_score, far_heads, preferred_element_type=jnp.float32
    )
    grad_values = jnp.einsum(
        "hqk,qhd->khd",
        probabilities.astype(jnp.bfloat16),
        far_grad_heads,
        preferred_element_type=jnp.float32,
    )
    scores = (
        jnp.einsum("qhd,khd->hqk", queries, panel_keys, preferred_element_type=jnp.float32)
        * scaling
    )
    probabilities = jnp.exp(jnp.where(visible, scores - log_total[:, :, None], MASKED_SCORE))
    grad_prob = jnp.einsum(
        "qhd,khd->hqk", grad_heads, split_panel[:, :, 1, :], preferred_element_type=jnp.float32
    )
    grad_score = (probabilities * (grad_prob - grad_dot[:, :, None]) * scaling).astype(jnp.bfloat16)
    grad_queries = jnp.einsum(
        "hqk,khd->qhd", grad_score, panel_keys, preferred_element_type=jnp.float32
    )
    grad_qkv = (
        jnp.stack([grad_queries, grad_keys, grad_values], axis=2)
        .astype(jnp.bfloat16)
        .reshape(local_rows, out_width)
    )
    partial_input = lax.dot_general(
        grad_qkv, weight, (((1,), (1,)), ((), ())), preferred_element_type=jnp.float32
    )
    grad_input = lax.psum_scatter(partial_input, "fsdp", scatter_dimension=1, tiled=True).astype(
        jnp.bfloat16
    )
    token_scale = (local_rows * seq_count) ** (-0.5)
    column_tokens = lax.all_to_all(tokens, "seq", split_axis=1, concat_axis=0, tiled=True)
    summed_rows = lax.dot_general(
        column_tokens,
        lax.all_gather(grad_qkv, "seq", axis=0, tiled=True),
        (((0,), (0,)), ((), ())),
        preferred_element_type=jnp.float32,
    )
    return (attention, grad_input, summed_rows * token_scale)


def dot(a, b):
    return lax.dot_general(a, b, (((1,), (0,)), ((), ())), preferred_element_type=F32)


def dot_nt(a, b):
    return lax.dot_general(a, b, (((1,), (1,)), ((), ())), preferred_element_type=F32)


def heads_kernel(slots, refs_of, where, *refs):
    named = dict(zip(refs_of, refs))
    covis, drive = named["covis"], named["drive"]
    t_all, w_all, gq = named["t_all"], named["w_all"], named["gq"]
    rows = BLOCK
    length = slots * rows
    z = lax.axis_index("seq")
    f = lax.axis_index("fsdp")
    y = lax.axis_index("groups")
    depth = w_all.shape[0] // slots
    half = depth // 2
    quarter = t_all.shape[1] // 4

    t_all[0:rows, :] = named["t0"][...]
    w_all[pl.ds(pl.multiple_of(z * depth, depth), depth), :] = named["w0"][...]
    width = w_all.shape[1]
    grads = [named["g0"][...]]
    for k in range(1, slots):
        name, at = where[k, "r"]
        r = named[name].at[pl.ds(at, rows), :]
        name, at = where[k, "v"]
        v = named[name].at[pl.ds(at, rows), :]
        first = (z ^ k) * depth
        w_all[pl.ds(pl.multiple_of(first + y * half, half), half), :] = r[:, 0:width]
        w_all[pl.ds(pl.multiple_of(first + (1 - y) * half, half), half), :] = v[...]
        pieces = [r[:, width : width + quarter]]
        for m in range(1, 4):
            name, at = where[k, m]
            pieces.append(named[name][pl.ds(at, rows), :])
        for m, piece in enumerate(pieces):
            columns = pl.ds(pl.multiple_of((f ^ m) * quarter, quarter), quarter)
            t_all[pl.ds(k * rows, rows), columns] = piece
        grads.append(r[:, width + quarter :])
    grads = jnp.concatenate(grads, axis=0)
    projected = dot(t_all[...], w_all[...]).astype(BF)
    grads_t = jnp.transpose(grads)

    bias = {}
    for a in range(slots):
        for b in range(slots):
            i, j = z ^ a, z ^ b
            seen = jnp.logical_or(covis[i, j] == 1, drive[i] == drive[j])
            bias[a, b] = jnp.where(seen, 0.0, MASKED_SCORE).astype(F32)

    heads = width // (3 * HD)
    span = 4 * rows
    out_columns = []
    attention_t = []
    for h in range(heads):
        base = 3 * HD * h
        q8 = projected[:, base : base + HD] * jnp.asarray(HD ** (-0.5), BF)
        k_h = projected[:, base + HD : base + 2 * HD]
        v_h = projected[:, base + 2 * HD : base + 3 * HD]
        k_t = jnp.transpose(k_h)
        v_t = jnp.transpose(v_h)
        g_h = grads[:, HD * h : HD * (h + 1)]
        g_t = grads_t[HD * h : HD * (h + 1), :]
        d_k = jnp.zeros((length, HD), F32)
        d_v = jnp.zeros((length, HD), F32)
        d_q_t = []
        for part in range(length // span):
            at = slice(part * span, (part + 1) * span)
            s_t = dot_nt(k_h, q8[at])
            masked = []
            for b in range(slots):
                masked.append(
                    jnp.concatenate(
                        [
                            s_t[b * rows : (b + 1) * rows, e * rows : (e + 1) * rows]
                            + bias[part * (span // rows) + e, b]
                            for e in range(span // rows)
                        ],
                        axis=1,
                    )
                )
            s_t = jnp.concatenate(masked, axis=0)
            top = jnp.max(s_t, axis=0, keepdims=True)
            e_t = jnp.exp(s_t - top)
            total = jnp.sum(e_t, axis=0, keepdims=True)
            p_t = e_t * (1.0 / total)
            p_b = p_t.astype(BF)
            p_rest = (p_t - p_b.astype(F32)).astype(BF)
            o_t = (dot(v_t, p_b) + dot(v_t, p_rest)).astype(BF)
            if part == 0:
                attention_t.append(o_t[:, 0:rows])
            grad_dot = jnp.sum(
                g_t[:, at].astype(F32) * o_t.astype(F32), axis=0, keepdims=True
            )
            dp_t = dot_nt(v_h, g_h[at])
            ds_t = (p_t * (dp_t - grad_dot)).astype(BF)
            d_v = d_v + dot(p_b, g_h[at])
            d_k = d_k + dot(ds_t, q8[at])
            d_q_t.append(dot(k_t, ds_t))
        d_q = jnp.transpose(jnp.concatenate(d_q_t, axis=1)) * (HD ** (-0.5))
        out_columns += [d_q, d_k, d_v]
    grad_qkv = jnp.concatenate(out_columns, axis=1).astype(BF)
    gq[...] = grad_qkv
    named["attention"][...] = jnp.transpose(jnp.concatenate(attention_t, axis=0))
    own = grad_qkv[0:rows]
    for m in range(4):
        out = named["part%d" % m]
        w_rows = w_all[pl.ds(pl.multiple_of((f ^ m) * depth, depth), depth), :]
        out[...] = dot_nt(own, w_rows).astype(out.dtype)
    named["t_d"][...] = t_all[:, pl.ds(pl.multiple_of(z * depth, depth), depth)]


def pack_kernel(w_ref, t_ref, g_ref, out, sems):
    half, width = out.shape[0], w_ref.shape[1]
    quarter = t_ref.shape[1] // 4
    y = lax.axis_index("groups")
    f = lax.axis_index("fsdp")
    copies = [
        pltpu.make_async_copy(
            w_ref.at[pl.ds(pl.multiple_of(y * half, half), half), :],
            out.at[:, pl.ds(0, width)],
            sems.at[0],
        ),
        pltpu.make_async_copy(
            t_ref.at[:, pl.ds(pl.multiple_of(f * quarter, quarter), quarter)],
            out.at[:, pl.ds(width, quarter)],
            sems.at[1],
        ),
        pltpu.make_async_copy(
            g_ref, out.at[:, pl.ds(width + quarter, g_ref.shape[1])], sems.at[2]
        ),
    ]
    for copy in copies:
        copy.start()
    for copy in copies:
        copy.wait()


def pack(tokens, qkv_weight, grad_out):
    rows, features = tokens.shape
    columns = qkv_weight.shape[1] + features // 4 + grad_out.shape[1]
    return pl.pallas_call(
        pack_kernel,
        out_shape=pltpu.VMEM((rows, columns), BF),
        in_specs=[pl.BlockSpec(memory_space=pl.ANY)] * 3,
        out_specs=pl.BlockSpec(memory_space=pltpu.VMEM),
        scratch_shapes=[pltpu.SemaphoreType.DMA((3,))],
        name="pack",
    )(qkv_weight, tokens, grad_out)


def short(tokens, qkv_weight, covisible, block_drive, grad_out):
    rows, features = tokens.shape
    slots = lax.axis_size("seq")
    z = lax.axis_index("seq")
    f = lax.axis_index("fsdp")
    y = lax.axis_index("groups")
    depth, width = qkv_weight.shape
    quarter = features // 4
    half = depth // 2

    def swap(x, axis, bit):
        n = lax.axis_size(axis)
        return lax.ppermute(x, axis, [(i, i ^ bit) for i in range(n)])

    packed = pack(tokens, qkv_weight, grad_out)
    got2 = swap(packed, "seq", 2)
    got1 = swap(packed, "seq", 1)
    got3 = swap(got2, "seq", 1)
    near = jnp.concatenate([got1, got2], axis=0)
    piece12 = near[:, width : width + quarter]
    piece3 = got3[:, width : width + quarter]
    x3 = swap(piece3, "fsdp", 2)
    v12 = swap(near[:, :width], "groups", 1)
    c3 = swap(piece3, "fsdp", 1)
    v3 = swap(got3[:, :width], "groups", 1)
    x12 = swap(piece12, "fsdp", 2)
    d3 = swap(piece3, "fsdp", 3)
    c12 = swap(piece12, "fsdp", 1)
    d12 = swap(piece12, "fsdp", 3)
    moved = dict(d12=d12, near=near, c3=c3, x3=x3, d3=d3, c12=c12, v3=v3, x12=x12, v12=v12, got3=got3)
    where = {}
    for k, at in ((1, 0), (2, rows)):
        where.update({(k, "r"): ("near", at), (k, "v"): ("v12", at)})
        where.update({(k, 1): ("c12", at), (k, 2): ("x12", at), (k, 3): ("d12", at)})
    where.update({(3, "r"): ("got3", 0), (3, "v"): ("v3", 0)})
    where.update({(3, 1): ("c3", 0), (3, 2): ("x3", 0), (3, 3): ("d3", 0)})
    names = ["covis", "drive", "t0", "w0", "g0"] + list(moved)
    values = [covisible, block_drive, tokens, qkv_weight, grad_out] + list(moved.values())
    outs = [
        ("attention", (rows, grad_out.shape[1]), BF),
        ("gq", (rows * slots, width), BF),
        ("t_d", (rows * slots, depth), BF),
        ("part0", (rows, depth), F32),
        ("part1", (rows, depth), BF),
        ("part2", (rows, depth), BF),
        ("part3", (rows, depth), BF),
    ]
    scratch = [
        ("t_all", pltpu.VMEM((rows * slots, features), BF)),
        ("w_all", pltpu.VMEM((depth * slots, width), BF)),
    ]
    vmem = pl.BlockSpec(memory_space=pltpu.VMEM)
    smem = pl.BlockSpec(memory_space=pltpu.SMEM)
    refs_of = names + [n for n, _, _ in outs] + [n for n, _ in scratch]
    attention, gq, t_d, *parts = pl.pallas_call(
        functools.partial(heads_kernel, slots, refs_of, where),
        out_shape=[pltpu.VMEM(s, d) for _, s, d in outs],
        in_specs=[smem, smem] + [vmem] * (len(names) - 2),
        out_specs=[vmem] * len(outs),
        scratch_shapes=[s for _, s in scratch],
        compiler_params=pltpu.CompilerParams(vmem_limit_bytes=48 << 20),
        name="heads",
    )(*values)
    total = parts[0]
    for m in (1, 2, 3):
        total = total + swap(parts[m], "fsdp", m).astype(F32)
    grad_input = total.astype(BF)
    grad_weight = lax.dot_general(
        t_d, gq, (((0,), (0,)), ((), ())), preferred_element_type=F32
    ) * ((rows * slots) ** (-0.5))
    return attention, grad_input, grad_weight


def per_device(tokens, qkv_weight, covisible, block_drive, grad_out):
    rows, features = tokens.shape
    depth = qkv_weight.shape[0]
    fits = (
        lax.axis_size("seq") == 4
        and lax.axis_size("fsdp") == 4
        and lax.axis_size("groups") == 2
        and rows == BLOCK
        and depth * 4 == features
        and depth == 2 * rows
    )
    body = short if fits else general
    return body(tokens, qkv_weight, covisible, block_drive, grad_out)


def solution(mesh):
    in_specs = (
        P(("groups", "seq"), None),
        P("seq", "fsdp"),
        P("groups", None),
        P("groups"),
        P(("groups", "seq"), "fsdp"),
    )
    out_specs = (
        P(("groups", "seq"), "fsdp"),
        P(("groups", "seq"), "fsdp"),
        P(("groups", "seq"), "fsdp"),
    )
    return jax.shard_map(
        per_device, mesh=mesh, in_specs=in_specs, out_specs=out_specs, check_vma=False
    )
```

```python
import functools
import jax
import jax.numpy as jnp
from jax import lax
from jax.experimental import pallas as pl
from jax.experimental.pallas import tpu as pltpu
from jax.sharding import PartitionSpec as P

HD = 64
BLOCK = 128
MASKED_SCORE = -1e30
BF = jnp.bfloat16
F32 = jnp.float32


def query_visible(covisible, block_drive, first_block, block_count):
    own_rows = lax.dynamic_slice_in_dim(covisible, first_block, block_count, 0)
    own_drive = lax.dynamic_slice_in_dim(block_drive, first_block, block_count, 0)
    joined = jnp.logical_or(own_rows == 1, own_drive[:, None] == block_drive[None, :])
    return joined.astype(jnp.float32)


def key_visible(covisible, block_drive, first_block, block_count):
    own_columns = lax.dynamic_slice_in_dim(covisible, first_block, block_count, 1)
    own_drive = lax.dynamic_slice_in_dim(block_drive, first_block, block_count, 0)
    joined = jnp.logical_or(own_columns == 1, block_drive[:, None] == own_drive[None, :])
    return joined.astype(jnp.float32)


def block_onehot(length, block_total):
    member = lax.iota(jnp.int32, length) // BLOCK
    return (member[:, None] == lax.iota(jnp.int32, block_total)[None, :]).astype(jnp.float32)


def general(tokens, qkv_weight, covisible, block_drive, grad_out):
    local_rows = tokens.shape[0]
    seq_count = lax.axis_size("seq")
    seq_index = lax.axis_index("seq")
    out_width = qkv_weight.shape[1]
    local_heads = out_width // (3 * HD)
    block_count = local_rows // BLOCK
    block_total = covisible.shape[0]
    first_block = seq_index * block_count
    scaling = HD ** (-0.5)
    rows_visible = query_visible(covisible, block_drive, first_block, block_count)
    columns_visible = key_visible(covisible, block_drive, first_block, block_count)
    weight = lax.all_gather(qkv_weight, "seq", axis=0, tiled=True)
    projected = jnp.dot(tokens, weight, preferred_element_type=jnp.float32)
    projected = projected.astype(jnp.bfloat16).reshape(local_rows, local_heads, 3, HD)
    queries = projected[:, :, 0, :]
    local_keys = projected[:, :, 1, :]
    local_values = projected[:, :, 2, :]
    key_value = projected[:, :, 1:, :].reshape(local_rows, local_heads * 2 * HD)
    panel = lax.all_gather(key_value, "seq", axis=0, tiled=True)
    length = panel.shape[0]
    onehot = block_onehot(length, block_total)
    visible = (jnp.repeat(jnp.dot(rows_visible, onehot.T), BLOCK, axis=0) > 0.5)[None]
    split_panel = panel.reshape(length, local_heads, 2, HD)
    panel_keys = split_panel[:, :, 0, :]
    scores = (
        jnp.einsum("qhd,khd->hqk", queries, panel_keys, preferred_element_type=jnp.float32)
        * scaling
    )
    running_max = jnp.where(visible, scores, MASKED_SCORE).max(axis=2)
    shifted = jnp.exp(jnp.where(visible, scores - running_max[:, :, None], MASKED_SCORE))
    running_sum = shifted.sum(axis=2)
    wide_values = split_panel[:, :, 1, :].astype(jnp.float32)
    weighted = jnp.einsum(
        "hqk,khd->hqd",
        shifted,
        wide_values,
        precision=lax.Precision.HIGHEST,
        preferred_element_type=jnp.float32,
    )
    attention_heads = (weighted / running_sum[:, :, None]).astype(jnp.bfloat16)
    attention = jnp.transpose(attention_heads, (1, 0, 2)).reshape(local_rows, local_heads * HD)
    log_total = running_max + jnp.log(running_sum)
    grad_heads = grad_out.reshape(local_rows, local_heads, HD)
    grad_dot_rows = jnp.sum(
        grad_heads.astype(jnp.float32)
        * attention.reshape(local_rows, local_heads, HD).astype(jnp.float32),
        axis=2,
    )
    grad_dot = jnp.transpose(grad_dot_rows)
    log_total_rows = jnp.transpose(log_total)
    all_log_total = lax.all_gather(log_total_rows, "seq", axis=0, tiled=True)
    all_grad_dot = lax.all_gather(grad_dot_rows, "seq", axis=0, tiled=True)
    query_rows = queries.reshape(local_rows, local_heads * HD)
    far_queries = lax.all_gather(query_rows, "seq", axis=0, tiled=True)
    far_grads = lax.all_gather(grad_out, "seq", axis=0, tiled=True)
    visible_columns = (jnp.repeat(jnp.dot(onehot, columns_visible), BLOCK, axis=1) > 0.5)[None]
    far_heads = far_queries.reshape(length, local_heads, HD)
    far_grad_heads = far_grads.reshape(length, local_heads, HD)
    far_log_total = jnp.transpose(all_log_total)
    far_grad_dot = jnp.transpose(all_grad_dot)
    scores = (
        jnp.einsum("qhd,khd->hqk", far_heads, local_keys, preferred_element_type=jnp.float32)
        * scaling
    )
    probabilities = jnp.exp(
        jnp.where(visible_columns, scores - far_log_total[:, :, None], MASKED_SCORE)
    )
    grad_prob = jnp.einsum(
        "qhd,khd->hqk", far_grad_heads, local_values, preferred_element_type=jnp.float32
    )
    grad_score = (probabilities * (grad_prob - far_grad_dot[:, :, None]) * scaling).astype(
        jnp.bfloat16
    )
    grad_keys = jnp.einsum(
        "hqk,qhd->khd", grad_score, far_heads, preferred_element_type=jnp.float32
    )
    grad_values = jnp.einsum(
        "hqk,qhd->khd",
        probabilities.astype(jnp.bfloat16),
        far_grad_heads,
        preferred_element_type=jnp.float32,
    )
    scores = (
        jnp.einsum("qhd,khd->hqk", queries, panel_keys, preferred_element_type=jnp.float32)
        * scaling
    )
    probabilities = jnp.exp(jnp.where(visible, scores - log_total[:, :, None], MASKED_SCORE))
    grad_prob = jnp.einsum(
        "qhd,khd->hqk", grad_heads, split_panel[:, :, 1, :], preferred_element_type=jnp.float32
    )
    grad_score = (probabilities * (grad_prob - grad_dot[:, :, None]) * scaling).astype(jnp.bfloat16)
    grad_queries = jnp.einsum(
        "hqk,khd->qhd", grad_score, panel_keys, preferred_element_type=jnp.float32
    )
    grad_qkv = (
        jnp.stack([grad_queries, grad_keys, grad_values], axis=2)
        .astype(jnp.bfloat16)
        .reshape(local_rows, out_width)
    )
    partial_input = lax.dot_general(
        grad_qkv, weight, (((1,), (1,)), ((), ())), preferred_element_type=jnp.float32
    )
    grad_input = lax.psum_scatter(partial_input, "fsdp", scatter_dimension=1, tiled=True).astype(
        jnp.bfloat16
    )
    token_scale = (local_rows * seq_count) ** (-0.5)
    column_tokens = lax.all_to_all(tokens, "seq", split_axis=1, concat_axis=0, tiled=True)
    summed_rows = lax.dot_general(
        column_tokens,
        lax.all_gather(grad_qkv, "seq", axis=0, tiled=True),
        (((0,), (0,)), ((), ())),
        preferred_element_type=jnp.float32,
    )
    return (attention, grad_input, summed_rows * token_scale)


def dot(a, b):
    return lax.dot_general(a, b, (((1,), (0,)), ((), ())), preferred_element_type=F32)


def dot_nt(a, b):
    return lax.dot_general(a, b, (((1,), (1,)), ((), ())), preferred_element_type=F32)


def heads_kernel(slots, refs_of, where, *refs):
    named = dict(zip(refs_of, refs))
    covis, drive = named["covis"], named["drive"]
    t_all, w_all = named["t_all"], named["w_all"]
    rows = BLOCK
    length = slots * rows
    z = lax.axis_index("seq")
    f = lax.axis_index("fsdp")
    depth = w_all.shape[0] // slots
    quarter = t_all.shape[1] // 4

    t_all[0:rows, :] = named["t0"][...]
    width = w_all.shape[1]
    grads = [named["g0"][...]]
    for k in range(1, slots):
        name, at, off = where[k, "t"]
        tg = named[name].at[pl.ds(at, rows), :]
        pieces = [tg[:, off : off + quarter]]
        for m in range(1, 4):
            name, at = where[k, m]
            pieces.append(named[name][pl.ds(at, rows), :])
        for m, piece in enumerate(pieces):
            columns = pl.ds(pl.multiple_of((f ^ m) * quarter, quarter), quarter)
            t_all[pl.ds(k * rows, rows), columns] = piece
        grads.append(tg[:, off + quarter :])
    grads = jnp.concatenate(grads, axis=0)
    projected = dot(t_all[...], w_all[...]).astype(BF)
    grads_t = jnp.transpose(grads)

    bias = {}
    for a in range(slots):
        for b in range(slots):
            i, j = z ^ a, z ^ b
            seen = jnp.logical_or(covis[i, j] == 1, drive[i] == drive[j])
            bias[a, b] = jnp.where(seen, 0.0, MASKED_SCORE).astype(F32)

    heads = width // (3 * HD)
    scale = HD ** (-0.5)
    bias_rows = [
        jnp.concatenate([jnp.full((1, rows), bias[a, b], F32) for a in range(slots)], axis=1)
        for b in range(slots)
    ]
    own = []
    for h in range(heads):
        q8, k_h, v_h = split_heads(projected, h)
        g_h = grads[:, HD * h : HD * (h + 1)]
        g_t = grads_t[HD * h : HD * (h + 1), :]
        s_t = dot_nt(k_h, q8)
        s_t = jnp.concatenate(
            [s_t[b * rows : (b + 1) * rows] + bias_rows[b] for b in range(slots)], axis=0
        )
        top = jnp.max(s_t, axis=0, keepdims=True)
        e_t = jnp.exp(s_t - top)
        total = jnp.sum(e_t, axis=0, keepdims=True)
        p_t = e_t * (1.0 / total)
        p_b = p_t.astype(BF)
        p_rest = (p_t - p_b.astype(F32)).astype(BF)
        v_t = jnp.transpose(v_h)
        o_t = (dot(v_t, p_b) + dot(v_t, p_rest)).astype(BF)
        grad_dot = jnp.sum(g_t.astype(F32) * o_t.astype(F32), axis=0, keepdims=True)
        named["p_b"][h] = p_b
        named["p_rest"][h] = p_rest
        named["grad_dot"][h] = grad_dot
        named["attention_t"][HD * h : HD * (h + 1), :] = o_t[:, 0:rows]
        ds_q = (p_t[:, 0:rows] * (dot_nt(v_h, g_h[0:rows]) - grad_dot[:, 0:rows])).astype(BF)
        ds_k = (p_t[0:rows] * (dot_nt(v_h[0:rows], g_h) - grad_dot)).astype(BF)
        d_q = jnp.transpose(dot(jnp.transpose(k_h), ds_q)) * scale
        own += [d_q, dot(ds_k, q8), dot(p_b[0:rows], g_h)]
    own = jnp.concatenate(own, axis=1).astype(BF)
    for m in range(4):
        out = named["part%d" % m]
        w_rows = w_all[pl.ds(pl.multiple_of((f ^ m) * depth, depth), depth), :]
        out[...] = dot_nt(own, w_rows).astype(out.dtype)
    named["projected"][...] = projected
    named["grads"][...] = grads
    named["t_d"][...] = t_all[:, pl.ds(pl.multiple_of(z * depth, depth), depth)]


def split_heads(projected, h):
    base = 3 * HD * h
    q8 = projected[:, base : base + HD] * jnp.asarray(HD ** (-0.5), BF)
    return q8, projected[:, base + HD : base + 2 * HD], projected[:, base + 2 * HD : base + 3 * HD]


def rest_kernel(
    p_b_ref, p_rest_ref, grad_dot_ref, attention_t, projected_ref, grads_ref, t_d, attention, weight
):
    projected, grads = projected_ref[...], grads_ref[...]
    columns = []
    for h in range(p_b_ref.shape[0]):
        q8, k_h, v_h = split_heads(projected, h)
        g_h = grads[:, HD * h : HD * (h + 1)]
        p_b = p_b_ref[h]
        p_t = p_b.astype(F32) + p_rest_ref[h].astype(F32)
        ds_t = (p_t * (dot_nt(v_h, g_h) - grad_dot_ref[h])).astype(BF)
        d_q = jnp.transpose(dot(jnp.transpose(k_h), ds_t)) * (HD ** (-0.5))
        columns += [d_q, dot(ds_t, q8), dot(p_b, g_h)]
    grad_qkv = jnp.concatenate(columns, axis=1).astype(BF)
    token_scale = grads.shape[0] ** (-0.5)
    weight[...] = dot(jnp.transpose(t_d[...]), grad_qkv) * token_scale
    attention[...] = jnp.transpose(attention_t[...])


def weight_kernel(slots, w0, near, far, near_half, far_half, out):
    z = lax.axis_index("seq")
    y = lax.axis_index("groups")
    depth, width = w0.shape
    half = depth // 2
    out[pl.ds(pl.multiple_of(z * depth, depth), depth), :] = w0[...]
    for k in range(1, slots):
        a, b, at = (far, far_half, 0) if k == 3 else (near, near_half, (k - 1) * half)
        first = (z ^ k) * depth
        out[pl.ds(pl.multiple_of(first + y * half, half), half), :] = a[at : at + half, 0:width]
        out[pl.ds(pl.multiple_of(first + (1 - y) * half, half), half), :] = b[at : at + half, :]


def pack_kernel(w_ref, t_ref, g_ref, out, sems):
    half, width = out.shape[0], w_ref.shape[1]
    quarter = t_ref.shape[1] // 4
    y = lax.axis_index("groups")
    f = lax.axis_index("fsdp")
    copies = [
        pltpu.make_async_copy(
            w_ref.at[pl.ds(pl.multiple_of(y * half, half), half), :],
            out.at[:, pl.ds(0, width)],
            sems.at[0],
        ),
        pltpu.make_async_copy(
            t_ref.at[:, pl.ds(pl.multiple_of(f * quarter, quarter), quarter)],
            out.at[:, pl.ds(width, quarter)],
            sems.at[1],
        ),
        pltpu.make_async_copy(
            g_ref, out.at[:, pl.ds(width + quarter, g_ref.shape[1])], sems.at[2]
        ),
    ]
    for copy in copies:
        copy.start()
    for copy in copies:
        copy.wait()


def pack(tokens, qkv_weight, grad_out):
    rows, features = tokens.shape
    columns = qkv_weight.shape[1] + features // 4 + grad_out.shape[1]
    return pl.pallas_call(
        pack_kernel,
        out_shape=pltpu.VMEM((rows, columns), BF),
        in_specs=[pl.BlockSpec(memory_space=pl.ANY)] * 3,
        out_specs=pl.BlockSpec(memory_space=pltpu.VMEM),
        scratch_shapes=[pltpu.SemaphoreType.DMA((3,))],
        name="pack",
    )(qkv_weight, tokens, grad_out)


def short(tokens, qkv_weight, covisible, block_drive, grad_out):
    rows, features = tokens.shape
    slots = lax.axis_size("seq")
    z = lax.axis_index("seq")
    f = lax.axis_index("fsdp")
    y = lax.axis_index("groups")
    depth, width = qkv_weight.shape
    quarter = features // 4
    half = depth // 2

    def swap(x, axis, bit):
        n = lax.axis_size(axis)
        return lax.ppermute(x, axis, [(i, i ^ bit) for i in range(n)])

    packed = pack(tokens, qkv_weight, grad_out)
    got2 = swap(packed, "seq", 2)
    got1 = swap(packed, "seq", 1)
    tg3 = swap(got2[:, width:], "seq", 1)
    got3 = swap(got2[:, :width], "seq", 1)
    near = jnp.concatenate([got1, got2], axis=0)
    piece12 = near[:, width : width + quarter]
    w12 = near[:, :width]
    piece3 = tg3[:, :quarter]
    w3 = got3
    v12 = swap(w12, "groups", 1)
    x12 = swap(piece12, "fsdp", 2)
    x3 = swap(piece3, "fsdp", 2)
    v3 = swap(w3, "groups", 1)
    call = swap(jnp.concatenate([piece12, x12, piece3, x3], axis=0), "fsdp", 1)
    vmem = pl.BlockSpec(memory_space=pltpu.VMEM)
    w_all = pl.pallas_call(
        functools.partial(weight_kernel, slots),
        out_shape=pltpu.VMEM((depth * slots, width), BF),
        in_specs=[vmem] * 5,
        out_specs=vmem,
        cost_estimate=pl.CostEstimate(flops=8000000000, transcendentals=0, bytes_accessed=2000000),
        compiler_params=pltpu.CompilerParams(vmem_limit_bytes=16 << 20),
        name="weight",
    )(qkv_weight, near, got3, v12, v3)
    moved = dict(near=near, tg3=tg3, x12=x12, x3=x3, call=call)
    where = {}
    for k, at in ((1, 0), (2, rows)):
        where.update({(k, "r"): ("near", at), (k, "t"): ("near", at, width), (k, "v"): ("v12", at)})
        where.update({(k, 1): ("call", at), (k, 2): ("x12", at), (k, 3): ("call", 2 * rows + at)})
    where.update({(3, "r"): ("got3", 0), (3, "t"): ("tg3", 0, 0), (3, "v"): ("v3", 0)})
    where.update({(3, 1): ("call", 4 * rows), (3, 2): ("x3", 0), (3, 3): ("call", 5 * rows)})
    names = ["covis", "drive", "t0", "g0", "w_all"] + list(moved)
    values = [covisible, block_drive, tokens, grad_out, w_all] + list(moved.values())
    heads = width // (3 * HD)
    length = rows * slots
    outs = [
        ("p_b", (heads, length, length), BF),
        ("p_rest", (heads, length, length), BF),
        ("grad_dot", (heads, 1, length), F32),
        ("attention_t", (heads * HD, rows), BF),
        ("projected", (length, width), BF),
        ("grads", (length, heads * HD), BF),
        ("t_d", (length, depth), BF),
        ("part0", (rows, depth), F32),
        ("part1", (rows, depth), BF),
        ("part2", (rows, depth), BF),
        ("part3", (rows, depth), BF),
    ]
    scratch = [
        ("t_all", pltpu.VMEM((rows * slots, features), BF)),
    ]
    vmem = pl.BlockSpec(memory_space=pltpu.VMEM)
    smem = pl.BlockSpec(memory_space=pltpu.SMEM)
    refs_of = names + [n for n, _, _ in outs] + [n for n, _ in scratch]
    *kept, part0, part1, part2, part3 = pl.pallas_call(
        functools.partial(heads_kernel, slots, refs_of, where),
        out_shape=[pltpu.VMEM(s, d) for _, s, d in outs],
        in_specs=[smem, smem] + [vmem] * (len(names) - 2),
        out_specs=[vmem] * len(outs),
        scratch_shapes=[s for _, s in scratch],
        compiler_params=pltpu.CompilerParams(vmem_limit_bytes=48 << 20),
        name="heads",
    )(*values)
    total = part0
    for m, part in ((1, part1), (2, part2), (3, part3)):
        total = total + swap(part, "fsdp", m).astype(F32)
    grad_input = total.astype(BF)
    attention, grad_weight = pl.pallas_call(
        rest_kernel,
        out_shape=[
            jax.ShapeDtypeStruct(grad_out.shape, BF),
            jax.ShapeDtypeStruct((depth, width), F32),
        ],
        in_specs=[vmem] * len(kept),
        out_specs=[vmem] * 2,
        compiler_params=pltpu.CompilerParams(vmem_limit_bytes=48 << 20),
        name="rest",
    )(*kept)
    return attention, grad_input, grad_weight


def per_device(tokens, qkv_weight, covisible, block_drive, grad_out):
    rows, features = tokens.shape
    depth = qkv_weight.shape[0]
    fits = (
        lax.axis_size("seq") == 4
        and lax.axis_size("fsdp") == 4
        and lax.axis_size("groups") == 2
        and rows == BLOCK
        and depth * 4 == features
        and depth == 2 * rows
    )
    body = short if fits else general
    return body(tokens, qkv_weight, covisible, block_drive, grad_out)


def solution(mesh):
    in_specs = (
        P(("groups", "seq"), None),
        P("seq", "fsdp"),
        P("groups", None),
        P("groups"),
        P(("groups", "seq"), "fsdp"),
    )
    out_specs = (
        P(("groups", "seq"), "fsdp"),
        P(("groups", "seq"), "fsdp"),
        P(("groups", "seq"), "fsdp"),
    )
    return jax.shard_map(
        per_device, mesh=mesh, in_specs=in_specs, out_specs=out_specs, check_vma=False
    )
```

```python
import functools
import jax
import jax.numpy as jnp
from jax import lax
from jax.experimental import pallas as pl
from jax.experimental.pallas import tpu as pltpu
from jax.sharding import PartitionSpec as P

HD = 64
BLOCK = 128
MASKED_SCORE = -1e30
BF = jnp.bfloat16
F32 = jnp.float32


def query_visible(covisible, block_drive, first_block, block_count):
    own_rows = lax.dynamic_slice_in_dim(covisible, first_block, block_count, 0)
    own_drive = lax.dynamic_slice_in_dim(block_drive, first_block, block_count, 0)
    joined = jnp.logical_or(own_rows == 1, own_drive[:, None] == block_drive[None, :])
    return joined.astype(jnp.float32)


def key_visible(covisible, block_drive, first_block, block_count):
    own_columns = lax.dynamic_slice_in_dim(covisible, first_block, block_count, 1)
    own_drive = lax.dynamic_slice_in_dim(block_drive, first_block, block_count, 0)
    joined = jnp.logical_or(own_columns == 1, block_drive[:, None] == own_drive[None, :])
    return joined.astype(jnp.float32)


def block_onehot(length, block_total):
    member = lax.iota(jnp.int32, length) // BLOCK
    return (member[:, None] == lax.iota(jnp.int32, block_total)[None, :]).astype(jnp.float32)


def general(tokens, qkv_weight, covisible, block_drive, grad_out):
    local_rows = tokens.shape[0]
    seq_count = lax.axis_size("seq")
    seq_index = lax.axis_index("seq")
    out_width = qkv_weight.shape[1]
    local_heads = out_width // (3 * HD)
    block_count = local_rows // BLOCK
    block_total = covisible.shape[0]
    first_block = seq_index * block_count
    scaling = HD ** (-0.5)
    rows_visible = query_visible(covisible, block_drive, first_block, block_count)
    columns_visible = key_visible(covisible, block_drive, first_block, block_count)
    weight = lax.all_gather(qkv_weight, "seq", axis=0, tiled=True)
    projected = jnp.dot(tokens, weight, preferred_element_type=jnp.float32)
    projected = projected.astype(jnp.bfloat16).reshape(local_rows, local_heads, 3, HD)
    queries = projected[:, :, 0, :]
    local_keys = projected[:, :, 1, :]
    local_values = projected[:, :, 2, :]
    key_value = projected[:, :, 1:, :].reshape(local_rows, local_heads * 2 * HD)
    panel = lax.all_gather(key_value, "seq", axis=0, tiled=True)
    length = panel.shape[0]
    onehot = block_onehot(length, block_total)
    visible = (jnp.repeat(jnp.dot(rows_visible, onehot.T), BLOCK, axis=0) > 0.5)[None]
    split_panel = panel.reshape(length, local_heads, 2, HD)
    panel_keys = split_panel[:, :, 0, :]
    scores = (
        jnp.einsum("qhd,khd->hqk", queries, panel_keys, preferred_element_type=jnp.float32)
        * scaling
    )
    running_max = jnp.where(visible, scores, MASKED_SCORE).max(axis=2)
    shifted = jnp.exp(jnp.where(visible, scores - running_max[:, :, None], MASKED_SCORE))
    running_sum = shifted.sum(axis=2)
    wide_values = split_panel[:, :, 1, :].astype(jnp.float32)
    weighted = jnp.einsum(
        "hqk,khd->hqd",
        shifted,
        wide_values,
        precision=lax.Precision.HIGHEST,
        preferred_element_type=jnp.float32,
    )
    attention_heads = (weighted / running_sum[:, :, None]).astype(jnp.bfloat16)
    attention = jnp.transpose(attention_heads, (1, 0, 2)).reshape(local_rows, local_heads * HD)
    log_total = running_max + jnp.log(running_sum)
    grad_heads = grad_out.reshape(local_rows, local_heads, HD)
    grad_dot_rows = jnp.sum(
        grad_heads.astype(jnp.float32)
        * attention.reshape(local_rows, local_heads, HD).astype(jnp.float32),
        axis=2,
    )
    grad_dot = jnp.transpose(grad_dot_rows)
    log_total_rows = jnp.transpose(log_total)
    all_log_total = lax.all_gather(log_total_rows, "seq", axis=0, tiled=True)
    all_grad_dot = lax.all_gather(grad_dot_rows, "seq", axis=0, tiled=True)
    query_rows = queries.reshape(local_rows, local_heads * HD)
    far_queries = lax.all_gather(query_rows, "seq", axis=0, tiled=True)
    far_grads = lax.all_gather(grad_out, "seq", axis=0, tiled=True)
    visible_columns = (jnp.repeat(jnp.dot(onehot, columns_visible), BLOCK, axis=1) > 0.5)[None]
    far_heads = far_queries.reshape(length, local_heads, HD)
    far_grad_heads = far_grads.reshape(length, local_heads, HD)
    far_log_total = jnp.transpose(all_log_total)
    far_grad_dot = jnp.transpose(all_grad_dot)
    scores = (
        jnp.einsum("qhd,khd->hqk", far_heads, local_keys, preferred_element_type=jnp.float32)
        * scaling
    )
    probabilities = jnp.exp(
        jnp.where(visible_columns, scores - far_log_total[:, :, None], MASKED_SCORE)
    )
    grad_prob = jnp.einsum(
        "qhd,khd->hqk", far_grad_heads, local_values, preferred_element_type=jnp.float32
    )
    grad_score = (probabilities * (grad_prob - far_grad_dot[:, :, None]) * scaling).astype(
        jnp.bfloat16
    )
    grad_keys = jnp.einsum(
        "hqk,qhd->khd", grad_score, far_heads, preferred_element_type=jnp.float32
    )
    grad_values = jnp.einsum(
        "hqk,qhd->khd",
        probabilities.astype(jnp.bfloat16),
        far_grad_heads,
        preferred_element_type=jnp.float32,
    )
    scores = (
        jnp.einsum("qhd,khd->hqk", queries, panel_keys, preferred_element_type=jnp.float32)
        * scaling
    )
    probabilities = jnp.exp(jnp.where(visible, scores - log_total[:, :, None], MASKED_SCORE))
    grad_prob = jnp.einsum(
        "qhd,khd->hqk", grad_heads, split_panel[:, :, 1, :], preferred_element_type=jnp.float32
    )
    grad_score = (probabilities * (grad_prob - grad_dot[:, :, None]) * scaling).astype(jnp.bfloat16)
    grad_queries = jnp.einsum(
        "hqk,khd->qhd", grad_score, panel_keys, preferred_element_type=jnp.float32
    )
    grad_qkv = (
        jnp.stack([grad_queries, grad_keys, grad_values], axis=2)
        .astype(jnp.bfloat16)
        .reshape(local_rows, out_width)
    )
    partial_input = lax.dot_general(
        grad_qkv, weight, (((1,), (1,)), ((), ())), preferred_element_type=jnp.float32
    )
    grad_input = lax.psum_scatter(partial_input, "fsdp", scatter_dimension=1, tiled=True).astype(
        jnp.bfloat16
    )
    token_scale = (local_rows * seq_count) ** (-0.5)
    column_tokens = lax.all_to_all(tokens, "seq", split_axis=1, concat_axis=0, tiled=True)
    summed_rows = lax.dot_general(
        column_tokens,
        lax.all_gather(grad_qkv, "seq", axis=0, tiled=True),
        (((0,), (0,)), ((), ())),
        preferred_element_type=jnp.float32,
    )
    return (attention, grad_input, summed_rows * token_scale)


def dot(a, b):
    return lax.dot_general(a, b, (((1,), (0,)), ((), ())), preferred_element_type=F32)


def dot_nt(a, b):
    return lax.dot_general(a, b, (((1,), (1,)), ((), ())), preferred_element_type=F32)


def heads_kernel(slots, refs_of, where, *refs):
    named = dict(zip(refs_of, refs))
    covis, drive = named["covis"], named["drive"]
    w_all = named["w_all"]
    rows = BLOCK
    length = slots * rows
    z = lax.axis_index("seq")
    f = lax.axis_index("fsdp")
    depth = w_all.shape[0] // slots
    quarter = depth

    width = w_all.shape[1]
    grads = [named["g0"][...]]
    pieces = [
        [named["t0"][:, pl.ds(pl.multiple_of((f ^ m) * quarter, quarter), quarter)]]
        for m in range(4)
    ]
    for k in range(1, slots):
        name, at, off = where[k, "t"]
        tg = named[name].at[pl.ds(at, rows), :]
        pieces[0].append(tg[:, off : off + quarter])
        for m in range(1, 4):
            name, at = where[k, m]
            pieces[m].append(named[name][pl.ds(at, rows), :])
        grads.append(tg[:, off + quarter :])
    grads = jnp.concatenate(grads, axis=0)
    projected = None
    for m in range(4):
        piece = jnp.concatenate(pieces[m], axis=0)
        named["pieces"][m] = piece
        term = dot(piece, w_all[pl.ds(pl.multiple_of((f ^ m) * quarter, quarter), quarter), :])
        projected = term if projected is None else projected + term
    projected = projected.astype(BF)
    grads_t = jnp.transpose(grads)

    bias = {}
    for a in range(slots):
        for b in range(slots):
            i, j = z ^ a, z ^ b
            seen = jnp.logical_or(covis[i, j] == 1, drive[i] == drive[j])
            bias[a, b] = jnp.where(seen, 0.0, MASKED_SCORE).astype(F32)

    heads = width // (3 * HD)
    scale = HD ** (-0.5)
    lane = lax.broadcasted_iota(jnp.int32, (rows, HD), 1)
    mark = [jnp.where(lane == b, 1.0, 0.0).astype(BF) for b in range(slots)]
    mark = jnp.concatenate(mark, axis=0)
    cost = []
    for a in range(slots):
        block = jnp.zeros((rows, HD), F32)
        for b in range(slots):
            block = jnp.where(lane == b, bias[a, b], block)
        cost.append(block.astype(BF))
    cost = jnp.concatenate(cost, axis=0)
    own = []
    state = []
    for h in range(heads):
        q8, k_h, v_h = split_heads(projected, h)
        g_h = grads[:, HD * h : HD * (h + 1)]
        g_t = grads_t[HD * h : HD * (h + 1), :]
        s_t = dot_nt(
            jnp.concatenate([k_h, mark], axis=1), jnp.concatenate([q8, cost], axis=1)
        )
        state.append((q8, k_h, v_h, g_h, g_t, s_t))
    more = []
    for h in range(heads):
        s_t = state[h][-1]
        top = jnp.max(s_t, axis=0, keepdims=True)
        e_t = jnp.exp(s_t - top)
        total = jnp.sum(e_t, axis=0, keepdims=True)
        p_t = e_t * (1.0 / total)
        p_b = p_t.astype(BF)
        p_rest = (p_t - p_b.astype(F32)).astype(BF)
        named["p_b"][h] = p_b
        named["p_rest"][h] = p_rest
        v_t = jnp.transpose(state[h][2])
        o_t = (dot(v_t, p_b) + dot(v_t, p_rest)).astype(BF)
        more.append((p_t[:, 0:rows], p_t[0:rows], p_b[0:rows], o_t))
    for h in range(heads):
        q8, k_h, v_h, g_h, g_t, _ = state[h]
        p_q, p_k, p_bk, o_t = more[h]
        grad_dot = jnp.sum(g_t.astype(F32) * o_t.astype(F32), axis=0, keepdims=True)
        named["grad_dot"][h] = grad_dot
        named["attention_t"][HD * h : HD * (h + 1), :] = o_t[:, 0:rows]
        ds_q = (p_q * (dot_nt(v_h, g_h[0:rows]) - grad_dot[:, 0:rows])).astype(BF)
        ds_k = (p_k * (dot_nt(v_h[0:rows], g_h) - grad_dot)).astype(BF)
        d_q = jnp.transpose(dot(jnp.transpose(k_h), ds_q)) * scale
        own += [d_q, dot(ds_k, q8), dot(p_bk, g_h)]
    own = jnp.concatenate(own, axis=1).astype(BF)
    for m in range(4):
        out = named["part%d" % m]
        w_rows = w_all[pl.ds(pl.multiple_of((f ^ m) * depth, depth), depth), :]
        out[...] = dot_nt(own, w_rows).astype(out.dtype)
    named["projected"][...] = projected
    named["grads"][...] = grads


def split_heads(projected, h):
    base = 3 * HD * h
    q8 = projected[:, base : base + HD] * jnp.asarray(HD ** (-0.5), BF)
    return q8, projected[:, base + HD : base + 2 * HD], projected[:, base + 2 * HD : base + 3 * HD]


def rest_kernel(
    p_b_ref, p_rest_ref, grad_dot_ref, attention_t, projected_ref, grads_ref, t_d, attention, weight
):
    projected, grads = projected_ref[...], grads_ref[...]
    columns = []
    for h in range(p_b_ref.shape[0]):
        q8, k_h, v_h = split_heads(projected, h)
        g_h = grads[:, HD * h : HD * (h + 1)]
        p_b = p_b_ref[h]
        p_t = p_b.astype(F32) + p_rest_ref[h].astype(F32)
        ds_t = (p_t * (dot_nt(v_h, g_h) - grad_dot_ref[h])).astype(BF)
        d_q = jnp.transpose(dot(jnp.transpose(k_h), ds_t)) * (HD ** (-0.5))
        columns += [d_q, dot(ds_t, q8), dot(p_b, g_h)]
    grad_qkv = jnp.concatenate(columns, axis=1).astype(BF)
    token_scale = grads.shape[0] ** (-0.5)
    weight[...] = dot(jnp.transpose(t_d[lax.axis_index("fsdp") ^ lax.axis_index("seq")]), grad_qkv) * token_scale
    attention[...] = jnp.transpose(attention_t[...])


def weight_kernel(slots, w0, near, far, near_half, far_half, out):
    z = lax.axis_index("seq")
    y = lax.axis_index("groups")
    depth, width = w0.shape
    half = depth // 2
    out[pl.ds(pl.multiple_of(z * depth, depth), depth), :] = w0[...]
    for k in range(1, slots):
        a, b, at = (far, far_half, 0) if k == 3 else (near, near_half, (k - 1) * half)
        first = (z ^ k) * depth
        out[pl.ds(pl.multiple_of(first + y * half, half), half), :] = a[at : at + half, 0:width]
        out[pl.ds(pl.multiple_of(first + (1 - y) * half, half), half), :] = b[at : at + half, :]


def pack_kernel(w_ref, t_ref, g_ref, out, sems):
    half, width = out.shape[0], w_ref.shape[1]
    quarter = t_ref.shape[1] // 4
    y = lax.axis_index("groups")
    f = lax.axis_index("fsdp")
    copies = [
        pltpu.make_async_copy(
            w_ref.at[pl.ds(pl.multiple_of(y * half, half), half), :],
            out.at[:, pl.ds(0, width)],
            sems.at[0],
        ),
        pltpu.make_async_copy(
            t_ref.at[:, pl.ds(pl.multiple_of(f * quarter, quarter), quarter)],
            out.at[:, pl.ds(width, quarter)],
            sems.at[1],
        ),
        pltpu.make_async_copy(
            g_ref, out.at[:, pl.ds(width + quarter, g_ref.shape[1])], sems.at[2]
        ),
    ]
    for copy in copies:
        copy.start()
    for copy in copies:
        copy.wait()


def pack(tokens, qkv_weight, grad_out):
    rows, features = tokens.shape
    columns = qkv_weight.shape[1] + features // 4 + grad_out.shape[1]
    return pl.pallas_call(
        pack_kernel,
        out_shape=pltpu.VMEM((rows, columns), BF),
        in_specs=[pl.BlockSpec(memory_space=pl.ANY)] * 3,
        out_specs=pl.BlockSpec(memory_space=pltpu.VMEM),
        scratch_shapes=[pltpu.SemaphoreType.DMA((3,))],
        name="pack",
    )(qkv_weight, tokens, grad_out)


def short(tokens, qkv_weight, covisible, block_drive, grad_out):
    rows, features = tokens.shape
    slots = lax.axis_size("seq")
    z = lax.axis_index("seq")
    f = lax.axis_index("fsdp")
    y = lax.axis_index("groups")
    depth, width = qkv_weight.shape
    quarter = features // 4
    half = depth // 2

    def swap(x, axis, bit):
        n = lax.axis_size(axis)
        return lax.ppermute(x, axis, [(i, i ^ bit) for i in range(n)])

    packed = pack(tokens, qkv_weight, grad_out)
    got2 = swap(packed, "seq", 2)
    got1 = swap(packed, "seq", 1)
    tg3 = swap(got2[:, width:], "seq", 1)
    got3 = swap(got2[:, :width], "seq", 1)
    near = jnp.concatenate([got1, got2], axis=0)
    piece12 = near[:, width : width + quarter]
    w12 = near[:, :width]
    piece3 = tg3[:, :quarter]
    w3 = got3
    v12 = swap(w12, "groups", 1)
    x12 = swap(piece12, "fsdp", 2)
    x3 = swap(piece3, "fsdp", 2)
    v3 = swap(w3, "groups", 1)
    call = swap(jnp.concatenate([piece12, x12, piece3, x3], axis=0), "fsdp", 1)
    vmem = pl.BlockSpec(memory_space=pltpu.VMEM)
    w_all = pl.pallas_call(
        functools.partial(weight_kernel, slots),
        out_shape=pltpu.VMEM((depth * slots, width), BF),
        in_specs=[vmem] * 5,
        out_specs=vmem,
        cost_estimate=pl.CostEstimate(flops=8000000000, transcendentals=0, bytes_accessed=2000000),
        compiler_params=pltpu.CompilerParams(vmem_limit_bytes=16 << 20),
        name="weight",
    )(qkv_weight, near, got3, v12, v3)
    moved = dict(near=near, tg3=tg3, x12=x12, x3=x3, call=call)
    where = {}
    for k, at in ((1, 0), (2, rows)):
        where.update({(k, "r"): ("near", at), (k, "t"): ("near", at, width), (k, "v"): ("v12", at)})
        where.update({(k, 1): ("call", at), (k, 2): ("x12", at), (k, 3): ("call", 2 * rows + at)})
    where.update({(3, "r"): ("got3", 0), (3, "t"): ("tg3", 0, 0), (3, "v"): ("v3", 0)})
    where.update({(3, 1): ("call", 4 * rows), (3, 2): ("x3", 0), (3, 3): ("call", 5 * rows)})
    names = ["covis", "drive", "t0", "g0", "w_all"] + list(moved)
    values = [covisible, block_drive, tokens, grad_out, w_all] + list(moved.values())
    heads = width // (3 * HD)
    length = rows * slots
    outs = [
        ("p_b", (heads, length, length), BF),
        ("p_rest", (heads, length, length), BF),
        ("grad_dot", (heads, 1, length), F32),
        ("attention_t", (heads * HD, rows), BF),
        ("projected", (length, width), BF),
        ("grads", (length, heads * HD), BF),
        ("pieces", (4, length, depth), BF),
        ("part0", (rows, depth), F32),
        ("part1", (rows, depth), BF),
        ("part2", (rows, depth), BF),
        ("part3", (rows, depth), BF),
    ]
    scratch = []
    vmem = pl.BlockSpec(memory_space=pltpu.VMEM)
    smem = pl.BlockSpec(memory_space=pltpu.SMEM)
    refs_of = names + [n for n, _, _ in outs] + [n for n, _ in scratch]
    *kept, part0, part1, part2, part3 = pl.pallas_call(
        functools.partial(heads_kernel, slots, refs_of, where),
        out_shape=[pltpu.VMEM(s, d) for _, s, d in outs],
        in_specs=[smem, smem] + [vmem] * (len(names) - 2),
        out_specs=[vmem] * len(outs),
        scratch_shapes=[s for _, s in scratch],
        compiler_params=pltpu.CompilerParams(vmem_limit_bytes=48 << 20),
        name="heads",
    )(*values)
    total = part0
    for m, part in ((1, part1), (2, part2), (3, part3)):
        total = total + swap(part, "fsdp", m).astype(F32)
    grad_input = total.astype(BF)
    attention, grad_weight = pl.pallas_call(
        rest_kernel,
        out_shape=[
            jax.ShapeDtypeStruct(grad_out.shape, BF),
            jax.ShapeDtypeStruct((depth, width), F32),
        ],
        in_specs=[vmem] * len(kept),
        out_specs=[vmem] * 2,
        compiler_params=pltpu.CompilerParams(vmem_limit_bytes=48 << 20),
        name="rest",
    )(*kept)
    return attention, grad_input, grad_weight


def per_device(tokens, qkv_weight, covisible, block_drive, grad_out):
    rows, features = tokens.shape
    depth = qkv_weight.shape[0]
    fits = (
        lax.axis_size("seq") == 4
        and lax.axis_size("fsdp") == 4
        and lax.axis_size("groups") == 2
        and rows == BLOCK
        and depth * 4 == features
        and depth == 2 * rows
    )
    body = short if fits else general
    return body(tokens, qkv_weight, covisible, block_drive, grad_out)


def solution(mesh):
    in_specs = (
        P(("groups", "seq"), None),
        P("seq", "fsdp"),
        P("groups", None),
        P("groups"),
        P(("groups", "seq"), "fsdp"),
    )
    out_specs = (
        P(("groups", "seq"), "fsdp"),
        P(("groups", "seq"), "fsdp"),
        P(("groups", "seq"), "fsdp"),
    )
    return jax.shard_map(
        per_device, mesh=mesh, in_specs=in_specs, out_specs=out_specs, check_vma=False
    )
```

```python
import functools
import jax
import jax.numpy as jnp
from jax import lax
from jax.experimental import pallas as pl
from jax.experimental.pallas import tpu as pltpu
from jax.sharding import PartitionSpec as P

HD = 64
BLOCK = 128
MASKED_SCORE = -1e30
BF = jnp.bfloat16
F32 = jnp.float32


def query_visible(covisible, block_drive, first_block, block_count):
    own_rows = lax.dynamic_slice_in_dim(covisible, first_block, block_count, 0)
    own_drive = lax.dynamic_slice_in_dim(block_drive, first_block, block_count, 0)
    joined = jnp.logical_or(own_rows == 1, own_drive[:, None] == block_drive[None, :])
    return joined.astype(jnp.float32)


def key_visible(covisible, block_drive, first_block, block_count):
    own_columns = lax.dynamic_slice_in_dim(covisible, first_block, block_count, 1)
    own_drive = lax.dynamic_slice_in_dim(block_drive, first_block, block_count, 0)
    joined = jnp.logical_or(own_columns == 1, block_drive[:, None] == own_drive[None, :])
    return joined.astype(jnp.float32)


def block_onehot(length, block_total):
    member = lax.iota(jnp.int32, length) // BLOCK
    return (member[:, None] == lax.iota(jnp.int32, block_total)[None, :]).astype(jnp.float32)


def general(tokens, qkv_weight, covisible, block_drive, grad_out):
    local_rows = tokens.shape[0]
    seq_count = lax.axis_size("seq")
    seq_index = lax.axis_index("seq")
    out_width = qkv_weight.shape[1]
    local_heads = out_width // (3 * HD)
    block_count = local_rows // BLOCK
    block_total = covisible.shape[0]
    first_block = seq_index * block_count
    scaling = HD ** (-0.5)
    rows_visible = query_visible(covisible, block_drive, first_block, block_count)
    columns_visible = key_visible(covisible, block_drive, first_block, block_count)
    weight = lax.all_gather(qkv_weight, "seq", axis=0, tiled=True)
    projected = jnp.dot(tokens, weight, preferred_element_type=jnp.float32)
    projected = projected.astype(jnp.bfloat16).reshape(local_rows, local_heads, 3, HD)
    queries = projected[:, :, 0, :]
    local_keys = projected[:, :, 1, :]
    local_values = projected[:, :, 2, :]
    key_value = projected[:, :, 1:, :].reshape(local_rows, local_heads * 2 * HD)
    panel = lax.all_gather(key_value, "seq", axis=0, tiled=True)
    length = panel.shape[0]
    onehot = block_onehot(length, block_total)
    visible = (jnp.repeat(jnp.dot(rows_visible, onehot.T), BLOCK, axis=0) > 0.5)[None]
    split_panel = panel.reshape(length, local_heads, 2, HD)
    panel_keys = split_panel[:, :, 0, :]
    scores = (
        jnp.einsum("qhd,khd->hqk", queries, panel_keys, preferred_element_type=jnp.float32)
        * scaling
    )
    running_max = jnp.where(visible, scores, MASKED_SCORE).max(axis=2)
    shifted = jnp.exp(jnp.where(visible, scores - running_max[:, :, None], MASKED_SCORE))
    running_sum = shifted.sum(axis=2)
    wide_values = split_panel[:, :, 1, :].astype(jnp.float32)
    weighted = jnp.einsum(
        "hqk,khd->hqd",
        shifted,
        wide_values,
        precision=lax.Precision.HIGHEST,
        preferred_element_type=jnp.float32,
    )
    attention_heads = (weighted / running_sum[:, :, None]).astype(jnp.bfloat16)
    attention = jnp.transpose(attention_heads, (1, 0, 2)).reshape(local_rows, local_heads * HD)
    log_total = running_max + jnp.log(running_sum)
    grad_heads = grad_out.reshape(local_rows, local_heads, HD)
    grad_dot_rows = jnp.sum(
        grad_heads.astype(jnp.float32)
        * attention.reshape(local_rows, local_heads, HD).astype(jnp.float32),
        axis=2,
    )
    grad_dot = jnp.transpose(grad_dot_rows)
    log_total_rows = jnp.transpose(log_total)
    all_log_total = lax.all_gather(log_total_rows, "seq", axis=0, tiled=True)
    all_grad_dot = lax.all_gather(grad_dot_rows, "seq", axis=0, tiled=True)
    query_rows = queries.reshape(local_rows, local_heads * HD)
    far_queries = lax.all_gather(query_rows, "seq", axis=0, tiled=True)
    far_grads = lax.all_gather(grad_out, "seq", axis=0, tiled=True)
    visible_columns = (jnp.repeat(jnp.dot(onehot, columns_visible), BLOCK, axis=1) > 0.5)[None]
    far_heads = far_queries.reshape(length, local_heads, HD)
    far_grad_heads = far_grads.reshape(length, local_heads, HD)
    far_log_total = jnp.transpose(all_log_total)
    far_grad_dot = jnp.transpose(all_grad_dot)
    scores = (
        jnp.einsum("qhd,khd->hqk", far_heads, local_keys, preferred_element_type=jnp.float32)
        * scaling
    )
    probabilities = jnp.exp(
        jnp.where(visible_columns, scores - far_log_total[:, :, None], MASKED_SCORE)
    )
    grad_prob = jnp.einsum(
        "qhd,khd->hqk", far_grad_heads, local_values, preferred_element_type=jnp.float32
    )
    grad_score = (probabilities * (grad_prob - far_grad_dot[:, :, None]) * scaling).astype(
        jnp.bfloat16
    )
    grad_keys = jnp.einsum(
        "hqk,qhd->khd", grad_score, far_heads, preferred_element_type=jnp.float32
    )
    grad_values = jnp.einsum(
        "hqk,qhd->khd",
        probabilities.astype(jnp.bfloat16),
        far_grad_heads,
        preferred_element_type=jnp.float32,
    )
    scores = (
        jnp.einsum("qhd,khd->hqk", queries, panel_keys, preferred_element_type=jnp.float32)
        * scaling
    )
    probabilities = jnp.exp(jnp.where(visible, scores - log_total[:, :, None], MASKED_SCORE))
    grad_prob = jnp.einsum(
        "qhd,khd->hqk", grad_heads, split_panel[:, :, 1, :], preferred_element_type=jnp.float32
    )
    grad_score = (probabilities * (grad_prob - grad_dot[:, :, None]) * scaling).astype(jnp.bfloat16)
    grad_queries = jnp.einsum(
        "hqk,khd->qhd", grad_score, panel_keys, preferred_element_type=jnp.float32
    )
    grad_qkv = (
        jnp.stack([grad_queries, grad_keys, grad_values], axis=2)
        .astype(jnp.bfloat16)
        .reshape(local_rows, out_width)
    )
    partial_input = lax.dot_general(
        grad_qkv, weight, (((1,), (1,)), ((), ())), preferred_element_type=jnp.float32
    )
    grad_input = lax.psum_scatter(partial_input, "fsdp", scatter_dimension=1, tiled=True).astype(
        jnp.bfloat16
    )
    token_scale = (local_rows * seq_count) ** (-0.5)
    column_tokens = lax.all_to_all(tokens, "seq", split_axis=1, concat_axis=0, tiled=True)
    summed_rows = lax.dot_general(
        column_tokens,
        lax.all_gather(grad_qkv, "seq", axis=0, tiled=True),
        (((0,), (0,)), ((), ())),
        preferred_element_type=jnp.float32,
    )
    return (attention, grad_input, summed_rows * token_scale)


def dot(a, b):
    return lax.dot_general(a, b, (((1,), (0,)), ((), ())), preferred_element_type=F32)


def dot_nt(a, b):
    return lax.dot_general(a, b, (((1,), (1,)), ((), ())), preferred_element_type=F32)


def heads_kernel(slots, refs_of, where, *refs):
    named = dict(zip(refs_of, refs))
    covis, drive = named["covis"], named["drive"]
    w_all = named["w_all"]
    rows = BLOCK
    length = slots * rows
    z = lax.axis_index("seq")
    f = lax.axis_index("fsdp")
    depth = w_all.shape[0] // slots
    quarter = depth

    width = w_all.shape[1]
    grads = [named["g0"][...]]
    pieces = [
        [named["t0"][:, pl.ds(pl.multiple_of((f ^ m) * quarter, quarter), quarter)]]
        for m in range(4)
    ]
    for k in range(1, slots):
        name, at, off = where[k, "t"]
        tg = named[name].at[pl.ds(at, rows), :]
        pieces[0].append(tg[:, off : off + quarter])
        for m in range(1, 4):
            name, at = where[k, m]
            pieces[m].append(named[name][pl.ds(at, rows), :])
        grads.append(tg[:, off + quarter :])
    grads = jnp.concatenate(grads, axis=0)
    projected = None
    for m in range(4):
        piece = jnp.concatenate(pieces[m], axis=0)
        named["pieces"][m] = piece
        term = dot(piece, w_all[pl.ds(pl.multiple_of((f ^ m) * quarter, quarter), quarter), :])
        projected = term if projected is None else projected + term
    projected = projected.astype(BF)
    grads_t = jnp.transpose(grads)

    bias = {}
    for a in range(slots):
        for b in range(slots):
            i, j = z ^ a, z ^ b
            seen = jnp.logical_or(covis[i, j] == 1, drive[i] == drive[j])
            bias[a, b] = jnp.where(seen, 0.0, MASKED_SCORE).astype(F32)

    heads = width // (3 * HD)
    scale = HD ** (-0.5)
    lane = lax.broadcasted_iota(jnp.int32, (rows, HD), 1)
    mark = [jnp.where(lane == b, 1.0, 0.0).astype(BF) for b in range(slots)]
    mark = jnp.concatenate(mark, axis=0)
    cost = []
    for a in range(slots):
        block = jnp.zeros((rows, HD), F32)
        for b in range(slots):
            block = jnp.where(lane == b, bias[a, b], block)
        cost.append(block.astype(BF))
    cost = jnp.concatenate(cost, axis=0)
    own = []
    state = []
    for h in range(heads):
        q8, k_h, v_h = split_heads(projected, h)
        g_h = grads[:, HD * h : HD * (h + 1)]
        g_t = grads_t[HD * h : HD * (h + 1), :]
        s_t = dot_nt(
            jnp.concatenate([k_h, mark], axis=1), jnp.concatenate([q8, cost], axis=1)
        )
        state.append((q8, k_h, v_h, g_h, g_t, s_t))
    more = []
    for h in range(heads):
        s_t = state[h][-1]
        top = jnp.max(s_t, axis=0, keepdims=True)
        e_t = jnp.exp(s_t - top)
        total = jnp.sum(e_t, axis=0, keepdims=True)
        p_t = e_t * (1.0 / total)
        p_b = p_t.astype(BF)
        p_rest = (p_t - p_b.astype(F32)).astype(BF)
        named["p_b"][h] = p_b
        named["p_rest"][h] = p_rest
        v_t = jnp.transpose(state[h][2])
        o_t = (dot(v_t, p_b) + dot(v_t, p_rest)).astype(BF)
        more.append((p_t[:, 0:rows], p_t[0:rows], p_b[0:rows], o_t))
    for h in range(heads):
        q8, k_h, v_h, g_h, g_t, _ = state[h]
        p_q, p_k, p_bk, o_t = more[h]
        grad_dot = jnp.sum(g_t.astype(F32) * o_t.astype(F32), axis=0, keepdims=True)
        named["grad_dot"][h] = grad_dot
        named["attention_t"][HD * h : HD * (h + 1), :] = o_t[:, 0:rows]
        ds_q = (p_q * (dot_nt(v_h, g_h[0:rows]) - grad_dot[:, 0:rows])).astype(BF)
        ds_k = (p_k * (dot_nt(v_h[0:rows], g_h) - grad_dot)).astype(BF)
        d_q = jnp.transpose(dot(jnp.transpose(k_h), ds_q)) * scale
        own += [d_q, dot(ds_k, q8), dot(p_bk, g_h)]
    own = jnp.concatenate(own, axis=1).astype(BF)
    for m in range(4):
        out = named["part%d" % m]
        w_rows = w_all[pl.ds(pl.multiple_of((f ^ m) * depth, depth), depth), :]
        out[...] = dot_nt(own, w_rows).astype(out.dtype)
    named["projected"][...] = projected
    named["grads"][...] = grads


def split_heads(projected, h):
    base = 3 * HD * h
    q8 = projected[:, base : base + HD] * jnp.asarray(HD ** (-0.5), BF)
    return q8, projected[:, base + HD : base + 2 * HD], projected[:, base + 2 * HD : base + 3 * HD]


def rest_kernel(
    p_b_ref, p_rest_ref, grad_dot_ref, attention_t, projected_ref, grads_ref, t_d, attention, weight
):
    projected, grads = projected_ref[...], grads_ref[...]
    columns = []
    heads = range(p_b_ref.shape[0])
    parts = [split_heads(projected, h) for h in heads]
    cotangents = [grads[:, HD * h : HD * (h + 1)] for h in heads]
    products = [dot_nt(parts[h][2], cotangents[h]) for h in heads]
    slopes = []
    for h in heads:
        p_t = p_b_ref[h].astype(F32) + p_rest_ref[h].astype(F32)
        slopes.append((p_t * (products[h] - grad_dot_ref[h])).astype(BF))
    for h in heads:
        q8, k_h, _ = parts[h]
        d_q = jnp.transpose(dot(jnp.transpose(k_h), slopes[h])) * (HD ** (-0.5))
        columns += [d_q, dot(slopes[h], q8), dot(p_b_ref[h], cotangents[h])]
    grad_qkv = jnp.concatenate(columns, axis=1).astype(BF)
    token_scale = grads.shape[0] ** (-0.5)
    weight[...] = dot(jnp.transpose(t_d[lax.axis_index("fsdp") ^ lax.axis_index("seq")]), grad_qkv) * token_scale
    attention[...] = jnp.transpose(attention_t[...])


def weight_kernel(slots, w0, near, far, near_half, far_half, out):
    z = lax.axis_index("seq")
    y = lax.axis_index("groups")
    depth, width = w0.shape
    half = depth // 2
    out[pl.ds(pl.multiple_of(z * depth, depth), depth), :] = w0[...]
    for k in range(1, slots):
        a, b, at = (far, far_half, 0) if k == 3 else (near, near_half, (k - 1) * half)
        first = (z ^ k) * depth
        out[pl.ds(pl.multiple_of(first + y * half, half), half), :] = a[at : at + half, 0:width]
        out[pl.ds(pl.multiple_of(first + (1 - y) * half, half), half), :] = b[at : at + half, :]


def pack_kernel(w_ref, t_ref, g_ref, out, sems):
    half, width = out.shape[0], w_ref.shape[1]
    quarter = t_ref.shape[1] // 4
    y = lax.axis_index("groups")
    f = lax.axis_index("fsdp")
    copies = [
        pltpu.make_async_copy(
            w_ref.at[pl.ds(pl.multiple_of(y * half, half), half), :],
            out.at[:, pl.ds(0, width)],
            sems.at[0],
        ),
        pltpu.make_async_copy(
            t_ref.at[:, pl.ds(pl.multiple_of(f * quarter, quarter), quarter)],
            out.at[:, pl.ds(width, quarter)],
            sems.at[1],
        ),
        pltpu.make_async_copy(
            g_ref, out.at[:, pl.ds(width + quarter, g_ref.shape[1])], sems.at[2]
        ),
    ]
    for copy in copies:
        copy.start()
    for copy in copies:
        copy.wait()


def pack(tokens, qkv_weight, grad_out):
    rows, features = tokens.shape
    columns = qkv_weight.shape[1] + features // 4 + grad_out.shape[1]
    return pl.pallas_call(
        pack_kernel,
        out_shape=pltpu.VMEM((rows, columns), BF),
        in_specs=[pl.BlockSpec(memory_space=pl.ANY)] * 3,
        out_specs=pl.BlockSpec(memory_space=pltpu.VMEM),
        scratch_shapes=[pltpu.SemaphoreType.DMA((3,))],
        name="pack",
    )(qkv_weight, tokens, grad_out)


def short(tokens, qkv_weight, covisible, block_drive, grad_out):
    rows, features = tokens.shape
    slots = lax.axis_size("seq")
    z = lax.axis_index("seq")
    f = lax.axis_index("fsdp")
    y = lax.axis_index("groups")
    depth, width = qkv_weight.shape
    quarter = features // 4
    half = depth // 2

    def swap(x, axis, bit):
        n = lax.axis_size(axis)
        return lax.ppermute(x, axis, [(i, i ^ bit) for i in range(n)])

    packed = pack(tokens, qkv_weight, grad_out)
    got2 = swap(packed, "seq", 2)
    got1 = swap(packed, "seq", 1)
    tg3 = swap(got2[:, width:], "seq", 1)
    got3 = swap(got2[:, :width], "seq", 1)
    near = jnp.concatenate([got1, got2], axis=0)
    piece12 = near[:, width : width + quarter]
    w12 = near[:, :width]
    piece3 = tg3[:, :quarter]
    w3 = got3
    v12 = swap(w12, "groups", 1)
    x12 = swap(piece12, "fsdp", 2)
    x3 = swap(piece3, "fsdp", 2)
    v3 = swap(w3, "groups", 1)
    call = swap(jnp.concatenate([piece12, x12, piece3, x3], axis=0), "fsdp", 1)
    vmem = pl.BlockSpec(memory_space=pltpu.VMEM)
    w_all = pl.pallas_call(
        functools.partial(weight_kernel, slots),
        out_shape=pltpu.VMEM((depth * slots, width), BF),
        in_specs=[vmem] * 5,
        out_specs=vmem,
        cost_estimate=pl.CostEstimate(flops=8000000000, transcendentals=0, bytes_accessed=2000000),
        compiler_params=pltpu.CompilerParams(vmem_limit_bytes=16 << 20),
        name="weight",
    )(qkv_weight, near, got3, v12, v3)
    moved = dict(near=near, tg3=tg3, x12=x12, x3=x3, call=call)
    where = {}
    for k, at in ((1, 0), (2, rows)):
        where.update({(k, "r"): ("near", at), (k, "t"): ("near", at, width), (k, "v"): ("v12", at)})
        where.update({(k, 1): ("call", at), (k, 2): ("x12", at), (k, 3): ("call", 2 * rows + at)})
    where.update({(3, "r"): ("got3", 0), (3, "t"): ("tg3", 0, 0), (3, "v"): ("v3", 0)})
    where.update({(3, 1): ("call", 4 * rows), (3, 2): ("x3", 0), (3, 3): ("call", 5 * rows)})
    names = ["covis", "drive", "t0", "g0", "w_all"] + list(moved)
    values = [covisible, block_drive, tokens, grad_out, w_all] + list(moved.values())
    heads = width // (3 * HD)
    length = rows * slots
    outs = [
        ("p_b", (heads, length, length), BF),
        ("p_rest", (heads, length, length), BF),
        ("grad_dot", (heads, 1, length), F32),
        ("attention_t", (heads * HD, rows), BF),
        ("projected", (length, width), BF),
        ("grads", (length, heads * HD), BF),
        ("pieces", (4, length, depth), BF),
        ("part0", (rows, depth), F32),
        ("part1", (rows, depth), BF),
        ("part2", (rows, depth), F32),
        ("part3", (rows, depth), BF),
    ]
    scratch = []
    vmem = pl.BlockSpec(memory_space=pltpu.VMEM)
    smem = pl.BlockSpec(memory_space=pltpu.SMEM)
    refs_of = names + [n for n, _, _ in outs] + [n for n, _ in scratch]
    *kept, part0, part1, part2, part3 = pl.pallas_call(
        functools.partial(heads_kernel, slots, refs_of, where),
        out_shape=[pltpu.VMEM(s, d) for _, s, d in outs],
        in_specs=[smem, smem] + [vmem] * (len(names) - 2),
        out_specs=[vmem] * len(outs),
        scratch_shapes=[s for _, s in scratch],
        compiler_params=pltpu.CompilerParams(vmem_limit_bytes=16 << 20),
        name="heads",
    )(*values)
    pair = (part2 + swap(part3, "fsdp", 1).astype(F32)).astype(BF)
    far = swap(pair, "fsdp", 2).astype(F32)
    grad_input = (part0 + swap(part1, "fsdp", 1).astype(F32) + far).astype(BF)
    attention, grad_weight = pl.pallas_call(
        rest_kernel,
        out_shape=[
            jax.ShapeDtypeStruct(grad_out.shape, BF),
            jax.ShapeDtypeStruct((depth, width), F32),
        ],
        in_specs=[vmem] * len(kept),
        out_specs=[vmem] * 2,
        compiler_params=pltpu.CompilerParams(vmem_limit_bytes=16 << 20),
        name="rest",
    )(*kept)
    return attention, grad_input, grad_weight


def per_device(tokens, qkv_weight, covisible, block_drive, grad_out):
    rows, features = tokens.shape
    depth = qkv_weight.shape[0]
    fits = (
        lax.axis_size("seq") == 4
        and lax.axis_size("fsdp") == 4
        and lax.axis_size("groups") == 2
        and rows == BLOCK
        and depth * 4 == features
        and depth == 2 * rows
    )
    body = short if fits else general
    return body(tokens, qkv_weight, covisible, block_drive, grad_out)


def solution(mesh):
    in_specs = (
        P(("groups", "seq"), None),
        P("seq", "fsdp"),
        P("groups", None),
        P("groups"),
        P(("groups", "seq"), "fsdp"),
    )
    out_specs = (
        P(("groups", "seq"), "fsdp"),
        P(("groups", "seq"), "fsdp"),
        P(("groups", "seq"), "fsdp"),
    )
    return jax.shard_map(
        per_device, mesh=mesh, in_specs=in_specs, out_specs=out_specs, check_vma=False
    )
```

```python
import functools
import jax
import jax.numpy as jnp
from jax import lax
from jax.experimental import pallas as pl
from jax.experimental.pallas import tpu as pltpu
from jax.sharding import PartitionSpec as P

HD = 64
BLOCK = 128
MASKED_SCORE = -1e30
BF = jnp.bfloat16
F32 = jnp.float32


def query_visible(covisible, block_drive, first_block, block_count):
    own_rows = lax.dynamic_slice_in_dim(covisible, first_block, block_count, 0)
    own_drive = lax.dynamic_slice_in_dim(block_drive, first_block, block_count, 0)
    joined = jnp.logical_or(own_rows == 1, own_drive[:, None] == block_drive[None, :])
    return joined.astype(jnp.float32)


def key_visible(covisible, block_drive, first_block, block_count):
    own_columns = lax.dynamic_slice_in_dim(covisible, first_block, block_count, 1)
    own_drive = lax.dynamic_slice_in_dim(block_drive, first_block, block_count, 0)
    joined = jnp.logical_or(own_columns == 1, block_drive[:, None] == own_drive[None, :])
    return joined.astype(jnp.float32)


def block_onehot(length, block_total):
    member = lax.iota(jnp.int32, length) // BLOCK
    return (member[:, None] == lax.iota(jnp.int32, block_total)[None, :]).astype(jnp.float32)


def general(tokens, qkv_weight, covisible, block_drive, grad_out):
    local_rows = tokens.shape[0]
    seq_count = lax.axis_size("seq")
    seq_index = lax.axis_index("seq")
    out_width = qkv_weight.shape[1]
    local_heads = out_width // (3 * HD)
    block_count = local_rows // BLOCK
    block_total = covisible.shape[0]
    first_block = seq_index * block_count
    scaling = HD ** (-0.5)
    rows_visible = query_visible(covisible, block_drive, first_block, block_count)
    columns_visible = key_visible(covisible, block_drive, first_block, block_count)
    weight = lax.all_gather(qkv_weight, "seq", axis=0, tiled=True)
    projected = jnp.dot(tokens, weight, preferred_element_type=jnp.float32)
    projected = projected.astype(jnp.bfloat16).reshape(local_rows, local_heads, 3, HD)
    queries = projected[:, :, 0, :]
    local_keys = projected[:, :, 1, :]
    local_values = projected[:, :, 2, :]
    key_value = projected[:, :, 1:, :].reshape(local_rows, local_heads * 2 * HD)
    panel = lax.all_gather(key_value, "seq", axis=0, tiled=True)
    length = panel.shape[0]
    onehot = block_onehot(length, block_total)
    visible = (jnp.repeat(jnp.dot(rows_visible, onehot.T), BLOCK, axis=0) > 0.5)[None]
    split_panel = panel.reshape(length, local_heads, 2, HD)
    panel_keys = split_panel[:, :, 0, :]
    scores = (
        jnp.einsum("qhd,khd->hqk", queries, panel_keys, preferred_element_type=jnp.float32)
        * scaling
    )
    running_max = jnp.where(visible, scores, MASKED_SCORE).max(axis=2)
    shifted = jnp.exp(jnp.where(visible, scores - running_max[:, :, None], MASKED_SCORE))
    running_sum = shifted.sum(axis=2)
    wide_values = split_panel[:, :, 1, :].astype(jnp.float32)
    weighted = jnp.einsum(
        "hqk,khd->hqd",
        shifted,
        wide_values,
        precision=lax.Precision.HIGHEST,
        preferred_element_type=jnp.float32,
    )
    attention_heads = (weighted / running_sum[:, :, None]).astype(jnp.bfloat16)
    attention = jnp.transpose(attention_heads, (1, 0, 2)).reshape(local_rows, local_heads * HD)
    log_total = running_max + jnp.log(running_sum)
    grad_heads = grad_out.reshape(local_rows, local_heads, HD)
    grad_dot_rows = jnp.sum(
        grad_heads.astype(jnp.float32)
        * attention.reshape(local_rows, local_heads, HD).astype(jnp.float32),
        axis=2,
    )
    grad_dot = jnp.transpose(grad_dot_rows)
    log_total_rows = jnp.transpose(log_total)
    all_log_total = lax.all_gather(log_total_rows, "seq", axis=0, tiled=True)
    all_grad_dot = lax.all_gather(grad_dot_rows, "seq", axis=0, tiled=True)
    query_rows = queries.reshape(local_rows, local_heads * HD)
    far_queries = lax.all_gather(query_rows, "seq", axis=0, tiled=True)
    far_grads = lax.all_gather(grad_out, "seq", axis=0, tiled=True)
    visible_columns = (jnp.repeat(jnp.dot(onehot, columns_visible), BLOCK, axis=1) > 0.5)[None]
    far_heads = far_queries.reshape(length, local_heads, HD)
    far_grad_heads = far_grads.reshape(length, local_heads, HD)
    far_log_total = jnp.transpose(all_log_total)
    far_grad_dot = jnp.transpose(all_grad_dot)
    scores = (
        jnp.einsum("qhd,khd->hqk", far_heads, local_keys, preferred_element_type=jnp.float32)
        * scaling
    )
    probabilities = jnp.exp(
        jnp.where(visible_columns, scores - far_log_total[:, :, None], MASKED_SCORE)
    )
    grad_prob = jnp.einsum(
        "qhd,khd->hqk", far_grad_heads, local_values, preferred_element_type=jnp.float32
    )
    grad_score = (probabilities * (grad_prob - far_grad_dot[:, :, None]) * scaling).astype(
        jnp.bfloat16
    )
    grad_keys = jnp.einsum(
        "hqk,qhd->khd", grad_score, far_heads, preferred_element_type=jnp.float32
    )
    grad_values = jnp.einsum(
        "hqk,qhd->khd",
        probabilities.astype(jnp.bfloat16),
        far_grad_heads,
        preferred_element_type=jnp.float32,
    )
    scores = (
        jnp.einsum("qhd,khd->hqk", queries, panel_keys, preferred_element_type=jnp.float32)
        * scaling
    )
    probabilities = jnp.exp(jnp.where(visible, scores - log_total[:, :, None], MASKED_SCORE))
    grad_prob = jnp.einsum(
        "qhd,khd->hqk", grad_heads, split_panel[:, :, 1, :], preferred_element_type=jnp.float32
    )
    grad_score = (probabilities * (grad_prob - grad_dot[:, :, None]) * scaling).astype(jnp.bfloat16)
    grad_queries = jnp.einsum(
        "hqk,khd->qhd", grad_score, panel_keys, preferred_element_type=jnp.float32
    )
    grad_qkv = (
        jnp.stack([grad_queries, grad_keys, grad_values], axis=2)
        .astype(jnp.bfloat16)
        .reshape(local_rows, out_width)
    )
    partial_input = lax.dot_general(
        grad_qkv, weight, (((1,), (1,)), ((), ())), preferred_element_type=jnp.float32
    )
    grad_input = lax.psum_scatter(partial_input, "fsdp", scatter_dimension=1, tiled=True).astype(
        jnp.bfloat16
    )
    token_scale = (local_rows * seq_count) ** (-0.5)
    column_tokens = lax.all_to_all(tokens, "seq", split_axis=1, concat_axis=0, tiled=True)
    summed_rows = lax.dot_general(
        column_tokens,
        lax.all_gather(grad_qkv, "seq", axis=0, tiled=True),
        (((0,), (0,)), ((), ())),
        preferred_element_type=jnp.float32,
    )
    return (attention, grad_input, summed_rows * token_scale)


def dot(a, b):
    return lax.dot_general(a, b, (((1,), (0,)), ((), ())), preferred_element_type=F32)


def dot_nt(a, b):
    return lax.dot_general(a, b, (((1,), (1,)), ((), ())), preferred_element_type=F32)


def heads_kernel(slots, refs_of, where, *refs):
    named = dict(zip(refs_of, refs))
    covis, drive = named["covis"], named["drive"]
    w_all = named["w_all"]
    rows = BLOCK
    length = slots * rows
    z = lax.axis_index("seq")
    f = lax.axis_index("fsdp")
    depth = w_all.shape[0] // slots
    quarter = depth

    width = w_all.shape[1]
    grads = [named["g0"][...]]
    pieces = [
        [named["t0"][:, pl.ds(pl.multiple_of((f ^ m) * quarter, quarter), quarter)]]
        for m in range(4)
    ]
    for k in range(1, slots):
        name, at, off = where[k, "t"]
        tg = named[name].at[pl.ds(at, rows), :]
        pieces[0].append(tg[:, off : off + quarter])
        for m in range(1, 4):
            name, at = where[k, m]
            pieces[m].append(named[name][pl.ds(at, rows), :])
        grads.append(tg[:, off + quarter :])
    grads = jnp.concatenate(grads, axis=0)
    projected = None
    for m in range(4):
        piece = jnp.concatenate(pieces[m], axis=0)
        named["pieces"][m] = piece
        term = dot(piece, w_all[pl.ds(pl.multiple_of((f ^ m) * quarter, quarter), quarter), :])
        projected = term if projected is None else projected + term
    projected = projected.astype(BF)
    grads_t = jnp.transpose(grads)

    bias = {}
    for a in range(slots):
        for b in range(slots):
            i, j = z ^ a, z ^ b
            seen = jnp.logical_or(covis[i, j] == 1, drive[i] == drive[j])
            bias[a, b] = jnp.where(seen, 0.0, MASKED_SCORE).astype(F32)

    heads = width // (3 * HD)
    scale = HD ** (-0.5)
    lane = lax.broadcasted_iota(jnp.int32, (rows, HD), 1)
    mark = [jnp.where(lane == b, 1.0, 0.0).astype(BF) for b in range(slots)]
    mark = jnp.concatenate(mark, axis=0)
    cost = []
    for a in range(slots):
        block = jnp.zeros((rows, HD), F32)
        for b in range(slots):
            block = jnp.where(lane == b, bias[a, b], block)
        cost.append(block.astype(BF))
    cost = jnp.concatenate(cost, axis=0)
    own = []
    state = []
    for h in range(heads):
        q8, k_h, v_h = split_heads(projected, h)
        g_h = grads[:, HD * h : HD * (h + 1)]
        g_t = grads_t[HD * h : HD * (h + 1), :]
        s_t = dot_nt(
            jnp.concatenate([k_h, mark], axis=1), jnp.concatenate([q8, cost], axis=1)
        )
        d_pq = dot_nt(v_h, g_h[0:rows])
        d_pk = dot_nt(v_h[0:rows], g_h)
        k_t, v_t = jnp.transpose(k_h), jnp.transpose(v_h)
        state.append((q8, k_t, d_pq, d_pk, v_t, g_h, g_t, s_t))
    more = []
    for h in range(heads):
        s_t = state[h][-1]
        top = jnp.max(s_t, axis=0, keepdims=True)
        e_t = jnp.exp(s_t - top)
        total = jnp.sum(e_t, axis=0, keepdims=True)
        p_t = e_t * (1.0 / total)
        p_b = p_t.astype(BF)
        p_rest = (p_t - p_b.astype(F32)).astype(BF)
        named["p_b"][h] = p_b
        named["p_rest"][h] = p_rest
        v_t = state[h][4]
        o_t = (dot(v_t, p_b) + dot(v_t, p_rest)).astype(BF)
        more.append((p_t[:, 0:rows], p_t[0:rows], p_b[0:rows], o_t))
    for h in range(heads):
        q8, k_t, d_pq, d_pk, _, g_h, g_t, _ = state[h]
        p_q, p_k, p_bk, o_t = more[h]
        grad_dot = jnp.sum(g_t.astype(F32) * o_t.astype(F32), axis=0, keepdims=True)
        named["grad_dot"][h] = grad_dot
        named["attention_t"][HD * h : HD * (h + 1), :] = o_t[:, 0:rows]
        ds_q = (p_q * (d_pq - grad_dot[:, 0:rows])).astype(BF)
        ds_k = (p_k * (d_pk - grad_dot)).astype(BF)
        d_q = jnp.transpose(dot(k_t, ds_q)) * scale
        own += [d_q, dot(ds_k, q8), dot(p_bk, g_h)]
    own = jnp.concatenate(own, axis=1).astype(BF)
    for m in range(4):
        out = named["part%d" % m]
        w_rows = w_all[pl.ds(pl.multiple_of((f ^ m) * depth, depth), depth), :]
        out[...] = dot_nt(own, w_rows).astype(out.dtype)
    named["projected"][...] = projected
    named["grads"][...] = grads


def split_heads(projected, h):
    base = 3 * HD * h
    q8 = projected[:, base : base + HD] * jnp.asarray(HD ** (-0.5), BF)
    return q8, projected[:, base + HD : base + 2 * HD], projected[:, base + 2 * HD : base + 3 * HD]


def rest_kernel(
    p_b_ref, p_rest_ref, grad_dot_ref, attention_t, projected_ref, grads_ref, t_d, attention, weight
):
    projected, grads = projected_ref[...], grads_ref[...]
    columns = []
    heads = range(p_b_ref.shape[0])
    parts = [split_heads(projected, h) for h in heads]
    cotangents = [grads[:, HD * h : HD * (h + 1)] for h in heads]
    products = [dot_nt(parts[h][2], cotangents[h]) for h in heads]
    slopes = []
    for h in heads:
        p_t = p_b_ref[h].astype(F32) + p_rest_ref[h].astype(F32)
        slopes.append((p_t * (products[h] - grad_dot_ref[h])).astype(BF))
    for h in heads:
        q8, k_h, _ = parts[h]
        d_q = jnp.transpose(dot(jnp.transpose(k_h), slopes[h])) * (HD ** (-0.5))
        columns += [d_q, dot(slopes[h], q8), dot(p_b_ref[h], cotangents[h])]
    grad_qkv = jnp.concatenate(columns, axis=1).astype(BF)
    token_scale = grads.shape[0] ** (-0.5)
    weight[...] = dot(jnp.transpose(t_d[lax.axis_index("fsdp") ^ lax.axis_index("seq")]), grad_qkv) * token_scale
    attention[...] = jnp.transpose(attention_t[...])


def weight_kernel(slots, w0, near, far, near_half, far_half, out):
    z = lax.axis_index("seq")
    y = lax.axis_index("groups")
    depth, width = w0.shape
    half = depth // 2
    out[pl.ds(pl.multiple_of(z * depth, depth), depth), :] = w0[...]
    for k in range(1, slots):
        a, b, at = (far, far_half, 0) if k == 3 else (near, near_half, (k - 1) * half)
        first = (z ^ k) * depth
        out[pl.ds(pl.multiple_of(first + y * half, half), half), :] = a[at : at + half, 0:width]
        out[pl.ds(pl.multiple_of(first + (1 - y) * half, half), half), :] = b[at : at + half, :]


def pack_kernel(w_ref, t_ref, g_ref, out, sems):
    half, width = out.shape[0], w_ref.shape[1]
    quarter = t_ref.shape[1] // 4
    y = lax.axis_index("groups")
    f = lax.axis_index("fsdp")
    copies = [
        pltpu.make_async_copy(
            w_ref.at[pl.ds(pl.multiple_of(y * half, half), half), :],
            out.at[:, pl.ds(0, width)],
            sems.at[0],
        ),
        pltpu.make_async_copy(
            t_ref.at[:, pl.ds(pl.multiple_of(f * quarter, quarter), quarter)],
            out.at[:, pl.ds(width, quarter)],
            sems.at[1],
        ),
        pltpu.make_async_copy(
            g_ref, out.at[:, pl.ds(width + quarter, g_ref.shape[1])], sems.at[2]
        ),
    ]
    for copy in copies:
        copy.start()
    for copy in copies:
        copy.wait()


def pack(tokens, qkv_weight, grad_out):
    rows, features = tokens.shape
    columns = qkv_weight.shape[1] + features // 4 + grad_out.shape[1]
    return pl.pallas_call(
        pack_kernel,
        out_shape=pltpu.VMEM((rows, columns), BF),
        in_specs=[pl.BlockSpec(memory_space=pl.ANY)] * 3,
        out_specs=pl.BlockSpec(memory_space=pltpu.VMEM),
        scratch_shapes=[pltpu.SemaphoreType.DMA((3,))],
        name="pack",
    )(qkv_weight, tokens, grad_out)


def short(tokens, qkv_weight, covisible, block_drive, grad_out):
    rows, features = tokens.shape
    slots = lax.axis_size("seq")
    z = lax.axis_index("seq")
    f = lax.axis_index("fsdp")
    y = lax.axis_index("groups")
    depth, width = qkv_weight.shape
    quarter = features // 4
    half = depth // 2

    def swap(x, axis, bit):
        n = lax.axis_size(axis)
        return lax.ppermute(x, axis, [(i, i ^ bit) for i in range(n)])

    packed = pack(tokens, qkv_weight, grad_out)
    got2 = swap(packed, "seq", 2)
    got1 = swap(packed, "seq", 1)
    tg3 = swap(got2[:, width:], "seq", 1)
    got3 = swap(got2[:, :width], "seq", 1)
    near = jnp.concatenate([got1, got2], axis=0)
    piece12 = near[:, width : width + quarter]
    w12 = near[:, :width]
    piece3 = tg3[:, :quarter]
    w3 = got3
    v12 = swap(w12, "groups", 1)
    x12 = swap(piece12, "fsdp", 2)
    x3 = swap(piece3, "fsdp", 2)
    v3 = swap(w3, "groups", 1)
    call = swap(jnp.concatenate([piece12, x12, piece3, x3], axis=0), "fsdp", 1)
    vmem = pl.BlockSpec(memory_space=pltpu.VMEM)
    w_all = pl.pallas_call(
        functools.partial(weight_kernel, slots),
        out_shape=pltpu.VMEM((depth * slots, width), BF),
        in_specs=[vmem] * 5,
        out_specs=vmem,
        cost_estimate=pl.CostEstimate(flops=8000000000, transcendentals=0, bytes_accessed=2000000),
        compiler_params=pltpu.CompilerParams(vmem_limit_bytes=16 << 20),
        name="weight",
    )(qkv_weight, near, got3, v12, v3)
    moved = dict(near=near, tg3=tg3, x12=x12, x3=x3, call=call)
    where = {}
    for k, at in ((1, 0), (2, rows)):
        where.update({(k, "r"): ("near", at), (k, "t"): ("near", at, width), (k, "v"): ("v12", at)})
        where.update({(k, 1): ("call", at), (k, 2): ("x12", at), (k, 3): ("call", 2 * rows + at)})
    where.update({(3, "r"): ("got3", 0), (3, "t"): ("tg3", 0, 0), (3, "v"): ("v3", 0)})
    where.update({(3, 1): ("call", 4 * rows), (3, 2): ("x3", 0), (3, 3): ("call", 5 * rows)})
    names = ["covis", "drive", "t0", "g0", "w_all"] + list(moved)
    values = [covisible, block_drive, tokens, grad_out, w_all] + list(moved.values())
    heads = width // (3 * HD)
    length = rows * slots
    outs = [
        ("p_b", (heads, length, length), BF),
        ("p_rest", (heads, length, length), BF),
        ("grad_dot", (heads, 1, length), F32),
        ("attention_t", (heads * HD, rows), BF),
        ("projected", (length, width), BF),
        ("grads", (length, heads * HD), BF),
        ("pieces", (4, length, depth), BF),
        ("part0", (rows, depth), F32),
        ("part1", (rows, depth), BF),
        ("part2", (rows, depth), F32),
        ("part3", (rows, depth), BF),
    ]
    scratch = []
    vmem = pl.BlockSpec(memory_space=pltpu.VMEM)
    smem = pl.BlockSpec(memory_space=pltpu.SMEM)
    refs_of = names + [n for n, _, _ in outs] + [n for n, _ in scratch]
    *kept, part0, part1, part2, part3 = pl.pallas_call(
        functools.partial(heads_kernel, slots, refs_of, where),
        out_shape=[pltpu.VMEM(s, d) for _, s, d in outs],
        in_specs=[smem, smem] + [vmem] * (len(names) - 2),
        out_specs=[vmem] * len(outs),
        scratch_shapes=[s for _, s in scratch],
        compiler_params=pltpu.CompilerParams(vmem_limit_bytes=16 << 20),
        name="heads",
    )(*values)
    pair = (part2 + swap(part3, "fsdp", 1).astype(F32)).astype(BF)
    far = swap(pair, "fsdp", 2).astype(F32)
    grad_input = (part0 + swap(part1, "fsdp", 1).astype(F32) + far).astype(BF)
    attention, grad_weight = pl.pallas_call(
        rest_kernel,
        out_shape=[
            jax.ShapeDtypeStruct(grad_out.shape, BF),
            jax.ShapeDtypeStruct((depth, width), F32),
        ],
        in_specs=[vmem] * len(kept),
        out_specs=[vmem] * 2,
        compiler_params=pltpu.CompilerParams(vmem_limit_bytes=16 << 20),
        name="rest",
    )(*kept)
    return attention, grad_input, grad_weight


def per_device(tokens, qkv_weight, covisible, block_drive, grad_out):
    rows, features = tokens.shape
    depth = qkv_weight.shape[0]
    fits = (
        lax.axis_size("seq") == 4
        and lax.axis_size("fsdp") == 4
        and lax.axis_size("groups") == 2
        and rows == BLOCK
        and depth * 4 == features
        and depth == 2 * rows
    )
    body = short if fits else general
    return body(tokens, qkv_weight, covisible, block_drive, grad_out)


def solution(mesh):
    in_specs = (
        P(("groups", "seq"), None),
        P("seq", "fsdp"),
        P("groups", None),
        P("groups"),
        P(("groups", "seq"), "fsdp"),
    )
    out_specs = (
        P(("groups", "seq"), "fsdp"),
        P(("groups", "seq"), "fsdp"),
        P(("groups", "seq"), "fsdp"),
    )
    return jax.shard_map(
        per_device, mesh=mesh, in_specs=in_specs, out_specs=out_specs, check_vma=False
    )
```

```python
import functools
import jax
import jax.numpy as jnp
from jax import lax
from jax.experimental import pallas as pl
from jax.experimental.pallas import tpu as pltpu
from jax.sharding import PartitionSpec as P

HD = 64
BLOCK = 128
MASKED_SCORE = -1e30
BF = jnp.bfloat16
F32 = jnp.float32


def query_visible(covisible, block_drive, first_block, block_count):
    own_rows = lax.dynamic_slice_in_dim(covisible, first_block, block_count, 0)
    own_drive = lax.dynamic_slice_in_dim(block_drive, first_block, block_count, 0)
    joined = jnp.logical_or(own_rows == 1, own_drive[:, None] == block_drive[None, :])
    return joined.astype(jnp.float32)


def key_visible(covisible, block_drive, first_block, block_count):
    own_columns = lax.dynamic_slice_in_dim(covisible, first_block, block_count, 1)
    own_drive = lax.dynamic_slice_in_dim(block_drive, first_block, block_count, 0)
    joined = jnp.logical_or(own_columns == 1, block_drive[:, None] == own_drive[None, :])
    return joined.astype(jnp.float32)


def block_onehot(length, block_total):
    member = lax.iota(jnp.int32, length) // BLOCK
    return (member[:, None] == lax.iota(jnp.int32, block_total)[None, :]).astype(jnp.float32)


def general(tokens, qkv_weight, covisible, block_drive, grad_out):
    local_rows = tokens.shape[0]
    seq_count = lax.axis_size("seq")
    seq_index = lax.axis_index("seq")
    out_width = qkv_weight.shape[1]
    local_heads = out_width // (3 * HD)
    block_count = local_rows // BLOCK
    block_total = covisible.shape[0]
    first_block = seq_index * block_count
    scaling = HD ** (-0.5)
    rows_visible = query_visible(covisible, block_drive, first_block, block_count)
    columns_visible = key_visible(covisible, block_drive, first_block, block_count)
    weight = lax.all_gather(qkv_weight, "seq", axis=0, tiled=True)
    projected = jnp.dot(tokens, weight, preferred_element_type=jnp.float32)
    projected = projected.astype(jnp.bfloat16).reshape(local_rows, local_heads, 3, HD)
    queries = projected[:, :, 0, :]
    local_keys = projected[:, :, 1, :]
    local_values = projected[:, :, 2, :]
    key_value = projected[:, :, 1:, :].reshape(local_rows, local_heads * 2 * HD)
    panel = lax.all_gather(key_value, "seq", axis=0, tiled=True)
    length = panel.shape[0]
    onehot = block_onehot(length, block_total)
    visible = (jnp.repeat(jnp.dot(rows_visible, onehot.T), BLOCK, axis=0) > 0.5)[None]
    split_panel = panel.reshape(length, local_heads, 2, HD)
    panel_keys = split_panel[:, :, 0, :]
    scores = (
        jnp.einsum("qhd,khd->hqk", queries, panel_keys, preferred_element_type=jnp.float32)
        * scaling
    )
    running_max = jnp.where(visible, scores, MASKED_SCORE).max(axis=2)
    shifted = jnp.exp(jnp.where(visible, scores - running_max[:, :, None], MASKED_SCORE))
    running_sum = shifted.sum(axis=2)
    wide_values = split_panel[:, :, 1, :].astype(jnp.float32)
    weighted = jnp.einsum(
        "hqk,khd->hqd",
        shifted,
        wide_values,
        precision=lax.Precision.HIGHEST,
        preferred_element_type=jnp.float32,
    )
    attention_heads = (weighted / running_sum[:, :, None]).astype(jnp.bfloat16)
    attention = jnp.transpose(attention_heads, (1, 0, 2)).reshape(local_rows, local_heads * HD)
    log_total = running_max + jnp.log(running_sum)
    grad_heads = grad_out.reshape(local_rows, local_heads, HD)
    grad_dot_rows = jnp.sum(
        grad_heads.astype(jnp.float32)
        * attention.reshape(local_rows, local_heads, HD).astype(jnp.float32),
        axis=2,
    )
    grad_dot = jnp.transpose(grad_dot_rows)
    log_total_rows = jnp.transpose(log_total)
    all_log_total = lax.all_gather(log_total_rows, "seq", axis=0, tiled=True)
    all_grad_dot = lax.all_gather(grad_dot_rows, "seq", axis=0, tiled=True)
    query_rows = queries.reshape(local_rows, local_heads * HD)
    far_queries = lax.all_gather(query_rows, "seq", axis=0, tiled=True)
    far_grads = lax.all_gather(grad_out, "seq", axis=0, tiled=True)
    visible_columns = (jnp.repeat(jnp.dot(onehot, columns_visible), BLOCK, axis=1) > 0.5)[None]
    far_heads = far_queries.reshape(length, local_heads, HD)
    far_grad_heads = far_grads.reshape(length, local_heads, HD)
    far_log_total = jnp.transpose(all_log_total)
    far_grad_dot = jnp.transpose(all_grad_dot)
    scores = (
        jnp.einsum("qhd,khd->hqk", far_heads, local_keys, preferred_element_type=jnp.float32)
        * scaling
    )
    probabilities = jnp.exp(
        jnp.where(visible_columns, scores - far_log_total[:, :, None], MASKED_SCORE)
    )
    grad_prob = jnp.einsum(
        "qhd,khd->hqk", far_grad_heads, local_values, preferred_element_type=jnp.float32
    )
    grad_score = (probabilities * (grad_prob - far_grad_dot[:, :, None]) * scaling).astype(
        jnp.bfloat16
    )
    grad_keys = jnp.einsum(
        "hqk,qhd->khd", grad_score, far_heads, preferred_element_type=jnp.float32
    )
    grad_values = jnp.einsum(
        "hqk,qhd->khd",
        probabilities.astype(jnp.bfloat16),
        far_grad_heads,
        preferred_element_type=jnp.float32,
    )
    scores = (
        jnp.einsum("qhd,khd->hqk", queries, panel_keys, preferred_element_type=jnp.float32)
        * scaling
    )
    probabilities = jnp.exp(jnp.where(visible, scores - log_total[:, :, None], MASKED_SCORE))
    grad_prob = jnp.einsum(
        "qhd,khd->hqk", grad_heads, split_panel[:, :, 1, :], preferred_element_type=jnp.float32
    )
    grad_score = (probabilities * (grad_prob - grad_dot[:, :, None]) * scaling).astype(jnp.bfloat16)
    grad_queries = jnp.einsum(
        "hqk,khd->qhd", grad_score, panel_keys, preferred_element_type=jnp.float32
    )
    grad_qkv = (
        jnp.stack([grad_queries, grad_keys, grad_values], axis=2)
        .astype(jnp.bfloat16)
        .reshape(local_rows, out_width)
    )
    partial_input = lax.dot_general(
        grad_qkv, weight, (((1,), (1,)), ((), ())), preferred_element_type=jnp.float32
    )
    grad_input = lax.psum_scatter(partial_input, "fsdp", scatter_dimension=1, tiled=True).astype(
        jnp.bfloat16
    )
    token_scale = (local_rows * seq_count) ** (-0.5)
    column_tokens = lax.all_to_all(tokens, "seq", split_axis=1, concat_axis=0, tiled=True)
    summed_rows = lax.dot_general(
        column_tokens,
        lax.all_gather(grad_qkv, "seq", axis=0, tiled=True),
        (((0,), (0,)), ((), ())),
        preferred_element_type=jnp.float32,
    )
    return (attention, grad_input, summed_rows * token_scale)


def dot(a, b):
    return lax.dot_general(a, b, (((1,), (0,)), ((), ())), preferred_element_type=F32)


def dot_nt(a, b):
    return lax.dot_general(a, b, (((1,), (1,)), ((), ())), preferred_element_type=F32)


def heads_kernel(slots, refs_of, where, *refs):
    named = dict(zip(refs_of, refs))
    covis, drive = named["covis"], named["drive"]
    w_all = named["w_all"]
    rows = BLOCK
    length = slots * rows
    z = lax.axis_index("seq")
    f = lax.axis_index("fsdp")
    depth = w_all.shape[0] // slots
    quarter = depth

    width = w_all.shape[1]
    grads = [named["g0"][...]]
    pieces = [
        [named["t0"][:, pl.ds(pl.multiple_of((f ^ m) * quarter, quarter), quarter)]]
        for m in range(4)
    ]
    for k in range(1, slots):
        name, at, off = where[k, "t"]
        tg = named[name].at[pl.ds(at, rows), :]
        pieces[0].append(tg[:, off : off + quarter])
        for m in range(1, 4):
            name, at = where[k, m]
            pieces[m].append(named[name][pl.ds(at, rows), :])
        grads.append(tg[:, off + quarter :])
    grads = jnp.concatenate(grads, axis=0)
    projected = None
    for m in range(4):
        piece = jnp.concatenate(pieces[m], axis=0)
        named["pieces"][m] = piece
        term = dot(piece, w_all[pl.ds(pl.multiple_of((f ^ m) * quarter, quarter), quarter), :])
        projected = term if projected is None else projected + term
    projected = projected.astype(BF)
    grads_t = jnp.transpose(grads)

    bias = {}
    for a in range(slots):
        for b in range(slots):
            i, j = z ^ a, z ^ b
            seen = jnp.logical_or(covis[i, j] == 1, drive[i] == drive[j])
            bias[a, b] = jnp.where(seen, 0.0, MASKED_SCORE).astype(F32)

    heads = width // (3 * HD)
    scale = HD ** (-0.5)
    lane = lax.broadcasted_iota(jnp.int32, (rows, HD), 1)
    mark = [jnp.where(lane == b, 1.0, 0.0).astype(BF) for b in range(slots)]
    mark = jnp.concatenate(mark, axis=0)
    cost = []
    for a in range(slots):
        block = jnp.zeros((rows, HD), F32)
        for b in range(slots):
            block = jnp.where(lane == b, bias[a, b], block)
        cost.append(block.astype(BF))
    cost = jnp.concatenate(cost, axis=0)
    own = []
    state = []
    for h in range(heads):
        q8, k_h, v_h = split_heads(projected, h)
        g_h = grads[:, HD * h : HD * (h + 1)]
        g_t = grads_t[HD * h : HD * (h + 1), :]
        s_t = dot_nt(
            jnp.concatenate([k_h, mark], axis=1), jnp.concatenate([q8, cost], axis=1)
        )
        d_pq = dot_nt(v_h, g_h[0:rows])
        d_pk = dot_nt(v_h[0:rows], g_h)
        k_t, v_t = jnp.transpose(k_h), jnp.transpose(v_h)
        state.append((q8, k_t, d_pq, d_pk, v_t, g_h, g_t, s_t))
    more = []
    for h in range(heads):
        s_t = state[h][-1]
        top = jnp.max(s_t, axis=0, keepdims=True)
        e_t = jnp.exp(s_t - top)
        total = jnp.sum(e_t, axis=0, keepdims=True)
        p_t = e_t * (1.0 / total)
        p_b = p_t.astype(BF)
        p_rest = (p_t - p_b.astype(F32)).astype(BF)
        named["p_b"][h] = p_b
        named["p_rest"][h] = p_rest
        v_t = state[h][4]
        o_t = (dot(v_t, p_b) + dot(v_t, p_rest)).astype(BF)
        more.append((p_t[:, 0:rows], p_t[0:rows], dot(p_b[0:rows], state[h][5]), o_t))
    for h in range(heads):
        q8, k_t, d_pq, d_pk, _, g_h, g_t, _ = state[h]
        p_q, p_k, p_bk, o_t = more[h]
        grad_dot = jnp.sum(g_t.astype(F32) * o_t.astype(F32), axis=0, keepdims=True)
        named["grad_dot"][h] = grad_dot
        named["attention_t"][HD * h : HD * (h + 1), :] = o_t[:, 0:rows]
        ds_q = (p_q * (d_pq - grad_dot[:, 0:rows])).astype(BF)
        ds_k = (p_k * (d_pk - grad_dot)).astype(BF)
        d_q = jnp.transpose(dot(k_t, ds_q)) * scale
        own += [d_q, dot(ds_k, q8), p_bk]
    own = jnp.concatenate(own, axis=1).astype(BF)
    for m in (3, 2, 1, 0):
        out = named["part%d" % m]
        w_rows = w_all[pl.ds(pl.multiple_of((f ^ m) * depth, depth), depth), :]
        out[...] = dot_nt(own, w_rows).astype(out.dtype)
    named["projected"][...] = projected
    named["grads"][...] = grads


def split_heads(projected, h):
    base = 3 * HD * h
    q8 = projected[:, base : base + HD] * jnp.asarray(HD ** (-0.5), BF)
    return q8, projected[:, base + HD : base + 2 * HD], projected[:, base + 2 * HD : base + 3 * HD]


def rest_kernel(
    p_b_ref, p_rest_ref, grad_dot_ref, attention_t, projected_ref, grads_ref, t_d, attention, weight
):
    projected, grads = projected_ref[...], grads_ref[...]
    columns = []
    heads = range(p_b_ref.shape[0])
    parts = [split_heads(projected, h) for h in heads]
    cotangents = [grads[:, HD * h : HD * (h + 1)] for h in heads]
    products = [dot_nt(parts[h][2], cotangents[h]) for h in heads]
    slopes = []
    for h in heads:
        p_t = p_b_ref[h].astype(F32) + p_rest_ref[h].astype(F32)
        slopes.append((p_t * (products[h] - grad_dot_ref[h])).astype(BF))
    for h in heads:
        q8, k_h, _ = parts[h]
        d_q = jnp.transpose(dot(jnp.transpose(k_h), slopes[h])) * (HD ** (-0.5))
        columns += [d_q, dot(slopes[h], q8), dot(p_b_ref[h], cotangents[h])]
    grad_qkv = jnp.concatenate(columns, axis=1).astype(BF)
    token_scale = grads.shape[0] ** (-0.5)
    weight[...] = dot(jnp.transpose(t_d[lax.axis_index("fsdp") ^ lax.axis_index("seq")]), grad_qkv) * token_scale
    attention[...] = jnp.transpose(attention_t[...])


def weight_kernel(slots, w0, near, far, near_half, far_half, out):
    z = lax.axis_index("seq")
    y = lax.axis_index("groups")
    depth, width = w0.shape
    half = depth // 2
    out[pl.ds(pl.multiple_of(z * depth, depth), depth), :] = w0[...]
    for k in range(1, slots):
        a, b, at = (far, far_half, 0) if k == 3 else (near, near_half, (k - 1) * half)
        first = (z ^ k) * depth
        out[pl.ds(pl.multiple_of(first + y * half, half), half), :] = a[at : at + half, 0:width]
        out[pl.ds(pl.multiple_of(first + (1 - y) * half, half), half), :] = b[at : at + half, :]


def pack_kernel(w_ref, t_ref, g_ref, out, sems):
    half, width = out.shape[0], w_ref.shape[1]
    quarter = t_ref.shape[1] // 4
    y = lax.axis_index("groups")
    f = lax.axis_index("fsdp")
    copies = [
        pltpu.make_async_copy(
            w_ref.at[pl.ds(pl.multiple_of(y * half, half), half), :],
            out.at[:, pl.ds(0, width)],
            sems.at[0],
        ),
        pltpu.make_async_copy(
            t_ref.at[:, pl.ds(pl.multiple_of(f * quarter, quarter), quarter)],
            out.at[:, pl.ds(width, quarter)],
            sems.at[1],
        ),
        pltpu.make_async_copy(
            g_ref, out.at[:, pl.ds(width + quarter, g_ref.shape[1])], sems.at[2]
        ),
    ]
    for copy in copies:
        copy.start()
    for copy in copies:
        copy.wait()


def pack(tokens, qkv_weight, grad_out):
    rows, features = tokens.shape
    columns = qkv_weight.shape[1] + features // 4 + grad_out.shape[1]
    return pl.pallas_call(
        pack_kernel,
        out_shape=pltpu.VMEM((rows, columns), BF),
        in_specs=[pl.BlockSpec(memory_space=pl.ANY)] * 3,
        out_specs=pl.BlockSpec(memory_space=pltpu.VMEM),
        scratch_shapes=[pltpu.SemaphoreType.DMA((3,))],
        name="pack",
    )(qkv_weight, tokens, grad_out)


def short(tokens, qkv_weight, covisible, block_drive, grad_out):
    rows, features = tokens.shape
    slots = lax.axis_size("seq")
    z = lax.axis_index("seq")
    f = lax.axis_index("fsdp")
    y = lax.axis_index("groups")
    depth, width = qkv_weight.shape
    quarter = features // 4
    half = depth // 2

    def swap(x, axis, bit):
        n = lax.axis_size(axis)
        return lax.ppermute(x, axis, [(i, i ^ bit) for i in range(n)])

    packed = pack(tokens, qkv_weight, grad_out)
    got2 = swap(packed, "seq", 2)
    got1 = swap(packed, "seq", 1)
    tg3 = swap(got2[:, width:], "seq", 1)
    got3 = swap(got2[:, :width], "seq", 1)
    near = jnp.concatenate([got1, got2], axis=0)
    piece12 = near[:, width : width + quarter]
    w12 = near[:, :width]
    piece3 = tg3[:, :quarter]
    w3 = got3
    v12 = swap(w12, "groups", 1)
    x12 = swap(piece12, "fsdp", 2)
    x3 = swap(piece3, "fsdp", 2)
    v3 = swap(w3, "groups", 1)
    call = swap(jnp.concatenate([piece12, x12, piece3, x3], axis=0), "fsdp", 1)
    vmem = pl.BlockSpec(memory_space=pltpu.VMEM)
    w_all = pl.pallas_call(
        functools.partial(weight_kernel, slots),
        out_shape=pltpu.VMEM((depth * slots, width), BF),
        in_specs=[vmem] * 5,
        out_specs=vmem,
        cost_estimate=pl.CostEstimate(flops=8000000000, transcendentals=0, bytes_accessed=2000000),
        compiler_params=pltpu.CompilerParams(vmem_limit_bytes=16 << 20),
        name="weight",
    )(qkv_weight, near, got3, v12, v3)
    moved = dict(near=near, tg3=tg3, x12=x12, x3=x3, call=call)
    where = {}
    for k, at in ((1, 0), (2, rows)):
        where.update({(k, "r"): ("near", at), (k, "t"): ("near", at, width), (k, "v"): ("v12", at)})
        where.update({(k, 1): ("call", at), (k, 2): ("x12", at), (k, 3): ("call", 2 * rows + at)})
    where.update({(3, "r"): ("got3", 0), (3, "t"): ("tg3", 0, 0), (3, "v"): ("v3", 0)})
    where.update({(3, 1): ("call", 4 * rows), (3, 2): ("x3", 0), (3, 3): ("call", 5 * rows)})
    names = ["covis", "drive", "t0", "g0", "w_all"] + list(moved)
    values = [covisible, block_drive, tokens, grad_out, w_all] + list(moved.values())
    heads = width // (3 * HD)
    length = rows * slots
    outs = [
        ("p_b", (heads, length, length), BF),
        ("p_rest", (heads, length, length), BF),
        ("grad_dot", (heads, 1, length), F32),
        ("attention_t", (heads * HD, rows), BF),
        ("projected", (length, width), BF),
        ("grads", (length, heads * HD), BF),
        ("pieces", (4, length, depth), BF),
        ("part0", (rows, depth), F32),
        ("part1", (rows, depth), BF),
        ("part2", (rows, depth), F32),
        ("part3", (rows, depth), BF),
    ]
    scratch = []
    vmem = pl.BlockSpec(memory_space=pltpu.VMEM)
    smem = pl.BlockSpec(memory_space=pltpu.SMEM)
    refs_of = names + [n for n, _, _ in outs] + [n for n, _ in scratch]
    *kept, part0, part1, part2, part3 = pl.pallas_call(
        functools.partial(heads_kernel, slots, refs_of, where),
        out_shape=[pltpu.VMEM(s, d) for _, s, d in outs],
        in_specs=[smem, smem] + [vmem] * (len(names) - 2),
        out_specs=[vmem] * len(outs),
        scratch_shapes=[s for _, s in scratch],
        compiler_params=pltpu.CompilerParams(vmem_limit_bytes=16 << 20),
        name="heads",
    )(*values)
    pair = (part2 + swap(part3, "fsdp", 1).astype(F32)).astype(BF)
    far = swap(pair, "fsdp", 2).astype(F32)
    grad_input = (part0 + swap(part1, "fsdp", 1).astype(F32) + far).astype(BF)
    attention, grad_weight = pl.pallas_call(
        rest_kernel,
        out_shape=[
            jax.ShapeDtypeStruct(grad_out.shape, BF),
            jax.ShapeDtypeStruct((depth, width), F32),
        ],
        in_specs=[vmem] * len(kept),
        out_specs=[vmem] * 2,
        compiler_params=pltpu.CompilerParams(vmem_limit_bytes=16 << 20),
        name="rest",
    )(*kept)
    return attention, grad_input, grad_weight


def per_device(tokens, qkv_weight, covisible, block_drive, grad_out):
    rows, features = tokens.shape
    depth = qkv_weight.shape[0]
    fits = (
        lax.axis_size("seq") == 4
        and lax.axis_size("fsdp") == 4
        and lax.axis_size("groups") == 2
        and rows == BLOCK
        and depth * 4 == features
        and depth == 2 * rows
    )
    body = short if fits else general
    return body(tokens, qkv_weight, covisible, block_drive, grad_out)


def solution(mesh):
    in_specs = (
        P(("groups", "seq"), None),
        P("seq", "fsdp"),
        P("groups", None),
        P("groups"),
        P(("groups", "seq"), "fsdp"),
    )
    out_specs = (
        P(("groups", "seq"), "fsdp"),
        P(("groups", "seq"), "fsdp"),
        P(("groups", "seq"), "fsdp"),
    )
    return jax.shard_map(
        per_device, mesh=mesh, in_specs=in_specs, out_specs=out_specs, check_vma=False
    )
```

```python
import functools
import jax
import jax.numpy as jnp
from jax import lax
from jax.experimental import pallas as pl
from jax.experimental.pallas import tpu as pltpu
from jax.sharding import PartitionSpec as P

HD = 64
BLOCK = 128
MASKED_SCORE = -1e30
BF = jnp.bfloat16
F32 = jnp.float32


def query_visible(covisible, block_drive, first_block, block_count):
    own_rows = lax.dynamic_slice_in_dim(covisible, first_block, block_count, 0)
    own_drive = lax.dynamic_slice_in_dim(block_drive, first_block, block_count, 0)
    joined = jnp.logical_or(own_rows == 1, own_drive[:, None] == block_drive[None, :])
    return joined.astype(jnp.float32)


def key_visible(covisible, block_drive, first_block, block_count):
    own_columns = lax.dynamic_slice_in_dim(covisible, first_block, block_count, 1)
    own_drive = lax.dynamic_slice_in_dim(block_drive, first_block, block_count, 0)
    joined = jnp.logical_or(own_columns == 1, block_drive[:, None] == own_drive[None, :])
    return joined.astype(jnp.float32)


def block_onehot(length, block_total):
    member = lax.iota(jnp.int32, length) // BLOCK
    return (member[:, None] == lax.iota(jnp.int32, block_total)[None, :]).astype(jnp.float32)


def general(tokens, qkv_weight, covisible, block_drive, grad_out):
    local_rows = tokens.shape[0]
    seq_count = lax.axis_size("seq")
    seq_index = lax.axis_index("seq")
    out_width = qkv_weight.shape[1]
    local_heads = out_width // (3 * HD)
    block_count = local_rows // BLOCK
    block_total = covisible.shape[0]
    first_block = seq_index * block_count
    scaling = HD ** (-0.5)
    rows_visible = query_visible(covisible, block_drive, first_block, block_count)
    columns_visible = key_visible(covisible, block_drive, first_block, block_count)
    weight = lax.all_gather(qkv_weight, "seq", axis=0, tiled=True)
    projected = jnp.dot(tokens, weight, preferred_element_type=jnp.float32)
    projected = projected.astype(jnp.bfloat16).reshape(local_rows, local_heads, 3, HD)
    queries = projected[:, :, 0, :]
    local_keys = projected[:, :, 1, :]
    local_values = projected[:, :, 2, :]
    key_value = projected[:, :, 1:, :].reshape(local_rows, local_heads * 2 * HD)
    panel = lax.all_gather(key_value, "seq", axis=0, tiled=True)
    length = panel.shape[0]
    onehot = block_onehot(length, block_total)
    visible = (jnp.repeat(jnp.dot(rows_visible, onehot.T), BLOCK, axis=0) > 0.5)[None]
    split_panel = panel.reshape(length, local_heads, 2, HD)
    panel_keys = split_panel[:, :, 0, :]
    scores = (
        jnp.einsum("qhd,khd->hqk", queries, panel_keys, preferred_element_type=jnp.float32)
        * scaling
    )
    running_max = jnp.where(visible, scores, MASKED_SCORE).max(axis=2)
    shifted = jnp.exp(jnp.where(visible, scores - running_max[:, :, None], MASKED_SCORE))
    running_sum = shifted.sum(axis=2)
    wide_values = split_panel[:, :, 1, :].astype(jnp.float32)
    weighted = jnp.einsum(
        "hqk,khd->hqd",
        shifted,
        wide_values,
        precision=lax.Precision.HIGHEST,
        preferred_element_type=jnp.float32,
    )
    attention_heads = (weighted / running_sum[:, :, None]).astype(jnp.bfloat16)
    attention = jnp.transpose(attention_heads, (1, 0, 2)).reshape(local_rows, local_heads * HD)
    log_total = running_max + jnp.log(running_sum)
    grad_heads = grad_out.reshape(local_rows, local_heads, HD)
    grad_dot_rows = jnp.sum(
        grad_heads.astype(jnp.float32)
        * attention.reshape(local_rows, local_heads, HD).astype(jnp.float32),
        axis=2,
    )
    grad_dot = jnp.transpose(grad_dot_rows)
    log_total_rows = jnp.transpose(log_total)
    all_log_total = lax.all_gather(log_total_rows, "seq", axis=0, tiled=True)
    all_grad_dot = lax.all_gather(grad_dot_rows, "seq", axis=0, tiled=True)
    query_rows = queries.reshape(local_rows, local_heads * HD)
    far_queries = lax.all_gather(query_rows, "seq", axis=0, tiled=True)
    far_grads = lax.all_gather(grad_out, "seq", axis=0, tiled=True)
    visible_columns = (jnp.repeat(jnp.dot(onehot, columns_visible), BLOCK, axis=1) > 0.5)[None]
    far_heads = far_queries.reshape(length, local_heads, HD)
    far_grad_heads = far_grads.reshape(length, local_heads, HD)
    far_log_total = jnp.transpose(all_log_total)
    far_grad_dot = jnp.transpose(all_grad_dot)
    scores = (
        jnp.einsum("qhd,khd->hqk", far_heads, local_keys, preferred_element_type=jnp.float32)
        * scaling
    )
    probabilities = jnp.exp(
        jnp.where(visible_columns, scores - far_log_total[:, :, None], MASKED_SCORE)
    )
    grad_prob = jnp.einsum(
        "qhd,khd->hqk", far_grad_heads, local_values, preferred_element_type=jnp.float32
    )
    grad_score = (probabilities * (grad_prob - far_grad_dot[:, :, None]) * scaling).astype(
        jnp.bfloat16
    )
    grad_keys = jnp.einsum(
        "hqk,qhd->khd", grad_score, far_heads, preferred_element_type=jnp.float32
    )
    grad_values = jnp.einsum(
        "hqk,qhd->khd",
        probabilities.astype(jnp.bfloat16),
        far_grad_heads,
        preferred_element_type=jnp.float32,
    )
    scores = (
        jnp.einsum("qhd,khd->hqk", queries, panel_keys, preferred_element_type=jnp.float32)
        * scaling
    )
    probabilities = jnp.exp(jnp.where(visible, scores - log_total[:, :, None], MASKED_SCORE))
    grad_prob = jnp.einsum(
        "qhd,khd->hqk", grad_heads, split_panel[:, :, 1, :], preferred_element_type=jnp.float32
    )
    grad_score = (probabilities * (grad_prob - grad_dot[:, :, None]) * scaling).astype(jnp.bfloat16)
    grad_queries = jnp.einsum(
        "hqk,khd->qhd", grad_score, panel_keys, preferred_element_type=jnp.float32
    )
    grad_qkv = (
        jnp.stack([grad_queries, grad_keys, grad_values], axis=2)
        .astype(jnp.bfloat16)
        .reshape(local_rows, out_width)
    )
    partial_input = lax.dot_general(
        grad_qkv, weight, (((1,), (1,)), ((), ())), preferred_element_type=jnp.float32
    )
    grad_input = lax.psum_scatter(partial_input, "fsdp", scatter_dimension=1, tiled=True).astype(
        jnp.bfloat16
    )
    token_scale = (local_rows * seq_count) ** (-0.5)
    column_tokens = lax.all_to_all(tokens, "seq", split_axis=1, concat_axis=0, tiled=True)
    summed_rows = lax.dot_general(
        column_tokens,
        lax.all_gather(grad_qkv, "seq", axis=0, tiled=True),
        (((0,), (0,)), ((), ())),
        preferred_element_type=jnp.float32,
    )
    return (attention, grad_input, summed_rows * token_scale)


def dot(a, b):
    return lax.dot_general(a, b, (((1,), (0,)), ((), ())), preferred_element_type=F32)


def dot_nt(a, b):
    return lax.dot_general(a, b, (((1,), (1,)), ((), ())), preferred_element_type=F32)


def heads_kernel(slots, refs_of, where, *refs):
    named = dict(zip(refs_of, refs))
    covis, drive = named["covis"], named["drive"]
    w_all = named["w_all"]
    rows = BLOCK
    length = slots * rows
    z = lax.axis_index("seq")
    f = lax.axis_index("fsdp")
    depth = w_all.shape[0] // slots
    quarter = depth

    width = w_all.shape[1]
    grads = [named["g0"][...]]
    pieces = [
        [named["t0"][:, pl.ds(pl.multiple_of((f ^ m) * quarter, quarter), quarter)]]
        for m in range(4)
    ]
    for k in range(1, slots):
        name, at, off = where[k, "t"]
        tg = named[name].at[pl.ds(at, rows), :]
        pieces[0].append(tg[:, off : off + quarter])
        for m in range(1, 4):
            name, at = where[k, m]
            pieces[m].append(named[name][pl.ds(at, rows), :])
        grads.append(tg[:, off + quarter :])
    grads = jnp.concatenate(grads, axis=0)
    projected = None
    for m in range(4):
        piece = jnp.concatenate(pieces[m], axis=0)
        named["pieces"][m] = piece
        term = dot(piece, w_all[pl.ds(pl.multiple_of((f ^ m) * quarter, quarter), quarter), :])
        projected = term if projected is None else projected + term
    projected = projected.astype(BF)
    grads_t = jnp.transpose(grads)

    bias = {}
    for a in range(slots):
        for b in range(slots):
            i, j = z ^ a, z ^ b
            seen = jnp.logical_or(covis[i, j] == 1, drive[i] == drive[j])
            bias[a, b] = jnp.where(seen, 0.0, MASKED_SCORE).astype(F32)

    heads = width // (3 * HD)
    scale = HD ** (-0.5)
    lane = lax.broadcasted_iota(jnp.int32, (rows, HD), 1)
    mark = [jnp.where(lane == b, 1.0, 0.0).astype(BF) for b in range(slots)]
    mark = jnp.concatenate(mark, axis=0)
    cost = []
    for a in range(slots):
        block = jnp.zeros((rows, HD), F32)
        for b in range(slots):
            block = jnp.where(lane == b, bias[a, b], block)
        cost.append(block.astype(BF))
    cost = jnp.concatenate(cost, axis=0)
    own = []
    state = []
    for h in range(heads):
        q8, k_h, v_h = split_heads(projected, h)
        g_h = grads[:, HD * h : HD * (h + 1)]
        g_t = grads_t[HD * h : HD * (h + 1), :]
        s_t = dot_nt(
            jnp.concatenate([k_h, mark], axis=1), jnp.concatenate([q8, cost], axis=1)
        )
        d_pq = dot_nt(v_h, g_h[0:rows])
        d_pk = dot_nt(v_h[0:rows], g_h)
        k_t, v_t = jnp.transpose(k_h), jnp.transpose(v_h)
        state.append((q8, k_t, d_pq, d_pk, v_t, g_h, g_t, s_t))
    more = []
    for h in range(heads):
        s_t = state[h][-1]
        top = jnp.max(s_t, axis=0, keepdims=True)
        e_t = jnp.exp(s_t - top)
        total = jnp.sum(e_t, axis=0, keepdims=True)
        p_t = e_t * (1.0 / total)
        p_b = p_t.astype(BF)
        p_rest = (p_t - p_b.astype(F32)).astype(BF)
        named["p_b"][h] = p_b
        named["p_rest"][h] = p_rest
        v_t = state[h][4]
        o_t = (dot(v_t, p_b) + dot(v_t, p_rest)).astype(BF)
        more.append((p_t[:, 0:rows], p_t[0:rows], dot(p_b[0:rows], state[h][5]), o_t))
    for h in range(heads):
        q8, k_t, d_pq, d_pk, _, g_h, g_t, _ = state[h]
        p_q, p_k, p_bk, o_t = more[h]
        grad_dot = jnp.sum(g_t.astype(F32) * o_t.astype(F32), axis=0, keepdims=True)
        named["grad_dot"][h] = grad_dot
        named["attention_t"][HD * h : HD * (h + 1), :] = o_t[:, 0:rows]
        ds_q = (p_q * (d_pq - grad_dot[:, 0:rows])).astype(BF)
        ds_k = (p_k * (d_pk - grad_dot)).astype(BF)
        d_q = jnp.transpose(dot(k_t, ds_q)) * scale
        own += [d_q, dot(ds_k, q8), p_bk]
    own = jnp.concatenate(own, axis=1).astype(BF)
    for m in (3, 2, 1, 0):
        out = named["part%d" % m]
        w_rows = w_all[pl.ds(pl.multiple_of((f ^ m) * depth, depth), depth), :]
        out[...] = dot_nt(own, w_rows).astype(out.dtype)
    named["projected"][...] = projected
    named["grads"][...] = grads


def split_heads(projected, h):
    base = 3 * HD * h
    q8 = projected[:, base : base + HD] * jnp.asarray(HD ** (-0.5), BF)
    return q8, projected[:, base + HD : base + 2 * HD], projected[:, base + 2 * HD : base + 3 * HD]


def rest_kernel(
    p_b_ref, p_rest_ref, grad_dot_ref, attention_t, projected_ref, grads_ref, t_d, attention, weight
):
    projected, grads = projected_ref[...], grads_ref[...]
    columns = []
    heads = range(p_b_ref.shape[0])
    parts = [split_heads(projected, h) for h in heads]
    cotangents = [grads[:, HD * h : HD * (h + 1)] for h in heads]
    products = [dot_nt(parts[h][2], cotangents[h]) for h in heads]
    slopes = []
    for h in heads:
        p_t = p_b_ref[h].astype(F32) + p_rest_ref[h].astype(F32)
        slopes.append((p_t * (products[h] - grad_dot_ref[h])).astype(BF))
    for h in heads:
        q8, k_h, _ = parts[h]
        d_q = jnp.transpose(dot(jnp.transpose(k_h), slopes[h])) * (HD ** (-0.5))
        columns += [d_q, dot(slopes[h], q8), dot(p_b_ref[h], cotangents[h])]
    grad_qkv = jnp.concatenate(columns, axis=1).astype(BF)
    token_scale = grads.shape[0] ** (-0.5)
    weight[...] = dot(jnp.transpose(t_d[lax.axis_index("fsdp") ^ lax.axis_index("seq")]), grad_qkv) * token_scale
    attention[...] = jnp.transpose(attention_t[...])


def weight_kernel(slots, w0, near, far, near_half, far_half, out):
    z = lax.axis_index("seq")
    y = lax.axis_index("groups")
    depth, width = w0.shape
    half = depth // 2
    out[pl.ds(pl.multiple_of(z * depth, depth), depth), :] = w0[...]
    for k in range(1, slots):
        a, b, at = (far, far_half, 0) if k == 3 else (near, near_half, (k - 1) * half)
        first = (z ^ k) * depth
        out[pl.ds(pl.multiple_of(first + y * half, half), half), :] = a[at : at + half, 0:width]
        out[pl.ds(pl.multiple_of(first + (1 - y) * half, half), half), :] = b[at : at + half, :]


def pack_kernel(w_ref, t_ref, g_ref, out, sems):
    half, width = out.shape[0], w_ref.shape[1]
    quarter = t_ref.shape[1] // 4
    y = lax.axis_index("groups")
    f = lax.axis_index("fsdp")
    copies = [
        pltpu.make_async_copy(
            w_ref.at[pl.ds(pl.multiple_of(y * half, half), half), :],
            out.at[:, pl.ds(0, width)],
            sems.at[0],
        ),
        pltpu.make_async_copy(
            t_ref.at[:, pl.ds(pl.multiple_of(f * quarter, quarter), quarter)],
            out.at[:, pl.ds(width, quarter)],
            sems.at[1],
        ),
        pltpu.make_async_copy(
            g_ref, out.at[:, pl.ds(width + quarter, g_ref.shape[1])], sems.at[2]
        ),
    ]
    for copy in copies:
        copy.start()
    for copy in copies:
        copy.wait()


def pack(tokens, qkv_weight, grad_out):
    rows, features = tokens.shape
    columns = qkv_weight.shape[1] + features // 4 + grad_out.shape[1]
    return pl.pallas_call(
        pack_kernel,
        out_shape=pltpu.VMEM((rows, columns), BF),
        in_specs=[pl.BlockSpec(memory_space=pl.ANY)] * 3,
        out_specs=pl.BlockSpec(memory_space=pltpu.VMEM),
        scratch_shapes=[pltpu.SemaphoreType.DMA((3,))],
        name="pack",
    )(qkv_weight, tokens, grad_out)


def short(tokens, qkv_weight, covisible, block_drive, grad_out):
    rows, features = tokens.shape
    slots = lax.axis_size("seq")
    z = lax.axis_index("seq")
    f = lax.axis_index("fsdp")
    y = lax.axis_index("groups")
    depth, width = qkv_weight.shape
    quarter = features // 4
    half = depth // 2

    def swap(x, axis, bit):
        n = lax.axis_size(axis)
        return lax.ppermute(x, axis, [(i, i ^ bit) for i in range(n)])

    packed = pack(tokens, qkv_weight, grad_out)
    got2 = swap(packed, "seq", 2)
    got1 = swap(packed, "seq", 1)
    tg3 = swap(got2[:, width:], "seq", 1)
    got3 = swap(got2[:, :width], "seq", 1)
    near = jnp.concatenate([got1, got2], axis=0)
    piece12 = near[:, width : width + quarter]
    w12 = near[:, :width]
    piece3 = tg3[:, :quarter]
    w3 = got3
    v12 = swap(w12, "groups", 1)
    x12 = swap(piece12, "fsdp", 2)
    x3 = swap(piece3, "fsdp", 2)
    v3 = swap(w3, "groups", 1)
    call = swap(jnp.concatenate([piece12, x12, piece3, x3], axis=0), "fsdp", 1)
    vmem = pl.BlockSpec(memory_space=pltpu.VMEM)
    w_all = pl.pallas_call(
        functools.partial(weight_kernel, slots),
        out_shape=pltpu.VMEM((depth * slots, width), BF),
        in_specs=[vmem] * 5,
        out_specs=vmem,
        cost_estimate=pl.CostEstimate(flops=8000000000, transcendentals=0, bytes_accessed=2000000),
        compiler_params=pltpu.CompilerParams(vmem_limit_bytes=16 << 20),
        name="weight",
    )(qkv_weight, near, got3, v12, v3)
    moved = dict(near=near, tg3=tg3, x12=x12, x3=x3, call=call)
    where = {}
    for k, at in ((1, 0), (2, rows)):
        where.update({(k, "r"): ("near", at), (k, "t"): ("near", at, width), (k, "v"): ("v12", at)})
        where.update({(k, 1): ("call", at), (k, 2): ("x12", at), (k, 3): ("call", 2 * rows + at)})
    where.update({(3, "r"): ("got3", 0), (3, "t"): ("tg3", 0, 0), (3, "v"): ("v3", 0)})
    where.update({(3, 1): ("call", 4 * rows), (3, 2): ("x3", 0), (3, 3): ("call", 5 * rows)})
    names = ["covis", "drive", "t0", "g0", "w_all"] + list(moved)
    values = [covisible, block_drive, tokens, grad_out, w_all] + list(moved.values())
    heads = width // (3 * HD)
    length = rows * slots
    outs = [
        ("p_b", (heads, length, length), BF),
        ("p_rest", (heads, length, length), BF),
        ("grad_dot", (heads, 1, length), F32),
        ("attention_t", (heads * HD, rows), BF),
        ("projected", (length, width), BF),
        ("grads", (length, heads * HD), BF),
        ("pieces", (4, length, depth), BF),
        ("part0", (rows, depth), F32),
        ("part1", (rows, depth), BF),
        ("part2", (rows, depth), BF),
        ("part3", (rows, depth), BF),
    ]
    scratch = []
    vmem = pl.BlockSpec(memory_space=pltpu.VMEM)
    smem = pl.BlockSpec(memory_space=pltpu.SMEM)
    refs_of = names + [n for n, _, _ in outs] + [n for n, _ in scratch]
    *kept, part0, part1, part2, part3 = pl.pallas_call(
        functools.partial(heads_kernel, slots, refs_of, where),
        out_shape=[pltpu.VMEM(s, d) for _, s, d in outs],
        in_specs=[smem, smem] + [vmem] * (len(names) - 2),
        out_specs=[vmem] * len(outs),
        scratch_shapes=[s for _, s in scratch],
        compiler_params=pltpu.CompilerParams(vmem_limit_bytes=16 << 20),
        name="heads",
    )(*values)
    total = part0
    for m, part in ((1, part1), (2, part2), (3, part3)):
        total = total + swap(part, "fsdp", m).astype(F32)
    grad_input = total.astype(BF)
    attention, grad_weight = pl.pallas_call(
        rest_kernel,
        out_shape=[
            jax.ShapeDtypeStruct(grad_out.shape, BF),
            jax.ShapeDtypeStruct((depth, width), F32),
        ],
        in_specs=[vmem] * len(kept),
        out_specs=[vmem] * 2,
        compiler_params=pltpu.CompilerParams(vmem_limit_bytes=16 << 20),
        name="rest",
    )(*kept)
    return attention, grad_input, grad_weight


def per_device(tokens, qkv_weight, covisible, block_drive, grad_out):
    rows, features = tokens.shape
    depth = qkv_weight.shape[0]
    fits = (
        lax.axis_size("seq") == 4
        and lax.axis_size("fsdp") == 4
        and lax.axis_size("groups") == 2
        and rows == BLOCK
        and depth * 4 == features
        and depth == 2 * rows
    )
    body = short if fits else general
    return body(tokens, qkv_weight, covisible, block_drive, grad_out)


def solution(mesh):
    in_specs = (
        P(("groups", "seq"), None),
        P("seq", "fsdp"),
        P("groups", None),
        P("groups"),
        P(("groups", "seq"), "fsdp"),
    )
    out_specs = (
        P(("groups", "seq"), "fsdp"),
        P(("groups", "seq"), "fsdp"),
        P(("groups", "seq"), "fsdp"),
    )
    return jax.shard_map(
        per_device, mesh=mesh, in_specs=in_specs, out_specs=out_specs, check_vma=False
    )
```
